32 devices in a mesh: az: 4 (over y, x), rng: 8 (over z, core).
Axes of the slice: x: 2, y: 2, z: 4, core: 2. Of those that a mesh axis runs over, the one named last changes fastest.
Arguments:
- echoes: bfloat16 [2, 256, 32, 1024], P(None, 'az', None, 'rng'), may hold values from -12 to 12
- arc_start: int32 [64], replicated, may hold values from 0 to 255, as said below
- arc_offsets: int32 [64, 16], replicated, may hold values from 0 to 63, as said below
- doppler_bins: int32 [64, 16], replicated, may hold values from 0 to 31
- steer_angles: float32 [64, 16], replicated, may hold values from -3.140625 to 3.140625
- train_mask: int32 [64, 8], P('az', 'rng'), may hold values from 0 to 1, as said below
Outputs:
- smoothed: float32 [64, 16, 1024], P('az', None, 'rng')
The draws below stay inside these ranges and needn't reach their ends.
Inputs may be any that keep to these rules, and one draw needn't show every extreme that they name: `arc_start`: beam b's arc begins at column (b * 4 - 64 / 2 + j) mod 256 for some j with 0 <= j < 4. `arc_offsets`: each row holds 16 distinct offsets, ascending. `train_mask`: the last block of every beam is a training block.
All inputs are finite; a program needn't handle non-finite values.
Results may differ from the reference program's by a relative error of at most 0.0035.
Values may be sent and summed in bfloat16 or wider, within the bound.
A program may use at most 64 MiB of HBM per device.

```python
import jax
import jax.numpy as jnp
from jax import lax

COLS = 256
PULSES = 32
ARC = 64
SEL = 16
BINS = 3
BEAMS = 64
DBINS = 16
BLK = 128
RANGE = 1024
NBLK = 8


PATCHES = 128


CLUTTER_LEVEL = 2.0


def clutter_steering(patch_key):
    jitter = jax.random.uniform(patch_key, (PATCHES,), jnp.float32, 0.0, 1.0)
    azimuth = 2.0 * jnp.pi * (jnp.arange(PATCHES, dtype=jnp.float32) + jitter) / PATCHES
    col_angle = 2.0 * jnp.pi * jnp.arange(COLS, dtype=jnp.float32) / COLS
    pulse_ids = jnp.arange(PULSES, dtype=jnp.float32)
    spatial = COLS / 2.0 * jnp.cos(col_angle[:, None, None] - azimuth[None, None, :])
    temporal = jnp.pi * jnp.cos(azimuth)[None, None, :] * pulse_ids[None, :, None]
    phase = (spatial + temporal).reshape(COLS * PULSES, PATCHES)
    return (jnp.cos(phase), jnp.sin(phase))


def clutter_field(steer_re, steer_im, amp_re, amp_im):
    real_part = jnp.dot(steer_re, amp_re, precision=lax.Precision.HIGHEST) - jnp.dot(steer_im, amp_im, precision=lax.Precision.HIGHEST)
    imag_part = jnp.dot(steer_re, amp_im, precision=lax.Precision.HIGHEST) + jnp.dot(steer_im, amp_re, precision=lax.Precision.HIGHEST)
    return jnp.stack([real_part, imag_part], 0).reshape(2, COLS, PULSES, RANGE)


def draw_echoes(key, part):
    base_key = jax.random.fold_in(key, 11)
    noise_key = jax.random.fold_in(base_key, 0)
    patch_key = jax.random.fold_in(base_key, 2)
    amp_key = jax.random.fold_in(base_key, 3)
    array_shape = (2, COLS, PULSES, RANGE)
    position = jnp.arange(RANGE, dtype=jnp.float32) / RANGE
    steer_re, steer_im = clutter_steering(patch_key)
    amp_scale = CLUTTER_LEVEL / PATCHES ** 0.5
    amplitudes = jax.random.normal(amp_key, (2, PATCHES, RANGE), jnp.float32) * amp_scale
    noise = jnp.clip(jax.random.normal(noise_key, array_shape, jnp.float32), -5.0, 5.0)
    values = noise + clutter_field(steer_re, steer_im, amplitudes[0], amplitudes[1])
    values = values * jnp.exp(0.6 * position)
    return jnp.clip(values, -12.0, 12.0).astype(jnp.bfloat16)


def draw_arc_start(key, part):
    spacing = COLS // BEAMS
    jitter = jax.random.randint(jax.random.fold_in(key, 12), (BEAMS,), 0, spacing)
    centre = jnp.arange(BEAMS, dtype=jnp.int32) * spacing
    return ((centre - ARC // 2 + jitter) % COLS).astype(jnp.int32)


def draw_arc_offsets(key, part):
    beam_keys = jax.random.split(jax.random.fold_in(key, 13), BEAMS)
    orders = jax.vmap(lambda single: jax.random.permutation(single, ARC))(beam_keys)
    return jnp.sort(orders[:, :SEL], axis=1).astype(jnp.int32)


def draw_train_mask(key, part):
    block_ids = jnp.arange(NBLK, dtype=jnp.int32)
    chance = 25 + 70 * block_ids // max(NBLK - 1, 1)
    rolls = jax.random.randint(jax.random.fold_in(key, 14), (BEAMS, NBLK), 0, 100)
    kept = jnp.where(block_ids[None, :] == NBLK - 1, 1, (rolls < chance[None, :]).astype(jnp.int32))
    return kept.astype(jnp.int32)


def plant(drawn, own_key, low, high):
    extent = drawn.shape
    spot = [jax.random.randint(jax.random.fold_in(own_key, axis), (), 0, extent[axis]) for axis in range(len(extent))]
    drawn = drawn.at[tuple(spot)].set(low)
    longest = extent.index(max(extent))
    spot[longest] = (spot[longest] + 1) % extent[longest]
    return drawn.at[tuple(spot)].set(high)


def setup_inputs(seed: int = 0) -> dict:
    arg_keys = jax.random.split(jax.random.key(seed), 7)
    return {
        "echoes": draw_echoes(jax.random.fold_in(arg_keys[6], 71), 0),
        "arc_start": draw_arc_start(jax.random.fold_in(arg_keys[6], 71), 0),
        "arc_offsets": draw_arc_offsets(jax.random.fold_in(arg_keys[6], 71), 0),
        "doppler_bins": plant(jax.random.randint(arg_keys[3], (BEAMS, DBINS), 0, PULSES), jax.random.fold_in(arg_keys[3], 1), 0, PULSES - 1).astype(jnp.int32),
        "steer_angles": jnp.clip(jax.random.uniform(arg_keys[4], (BEAMS, SEL), jnp.float32, -3.140625, 3.140625), -3.140625, 3.140625),
        "train_mask": draw_train_mask(jax.random.fold_in(arg_keys[6], 71), 0),
    }


LOADING = 0.1

def doppler_table():
    freq_ids = jnp.arange(PULSES, dtype=jnp.int32)
    phase_steps = freq_ids[:, None] * freq_ids[None, :] % PULSES
    phase_angle = -2.0 * jnp.pi / PULSES * phase_steps.astype(jnp.float32)
    return (jnp.cos(phase_angle).astype(jnp.bfloat16), jnp.sin(phase_angle).astype(jnp.bfloat16))

def snapshot(beam_cols, centers, beam_angle, table_re, table_im):
    num_sel = beam_cols.shape[1]
    num_pulses = beam_cols.shape[2]
    num_cells = beam_cols.shape[3]
    num_chan = centers.shape[0]
    bin_ids = ((centers[:, None] + jnp.arange(BINS, dtype=jnp.int32)[None, :] - BINS // 2) % num_pulses).reshape(-1)
    bin_pick = (jnp.arange(num_pulses, dtype=jnp.int32)[None, :] == bin_ids[:, None]).astype(jnp.bfloat16)
    wt_real = jnp.dot(bin_pick.astype(jnp.float32), table_re.astype(jnp.float32), preferred_element_type=jnp.float32).astype(jnp.bfloat16)
    wt_imag = jnp.dot(bin_pick.astype(jnp.float32), table_im.astype(jnp.float32), preferred_element_type=jnp.float32).astype(jnp.bfloat16)
    stacked_table = jnp.concatenate([jnp.concatenate([wt_real, -wt_imag], 1), jnp.concatenate([wt_imag, wt_real], 1)], 0)
    flat_cols = jnp.transpose(beam_cols, (0, 2, 1, 3)).reshape(2 * num_pulses, num_sel * num_cells)
    spectrum = jnp.dot(stacked_table.astype(jnp.float32), flat_cols.astype(jnp.float32), preferred_element_type=jnp.float32).reshape(2, num_chan, BINS, num_sel, num_cells)
    cosine = jnp.cos(beam_angle)[None, None, :, None]
    sine_part = jnp.sin(beam_angle)[None, None, :, None]
    part_real = cosine * spectrum[0] - sine_part * spectrum[1]
    part_imag = sine_part * spectrum[0] + cosine * spectrum[1]
    joined = jnp.concatenate([part_real.reshape(num_chan, BINS * num_sel, num_cells), part_imag.reshape(num_chan, BINS * num_sel, num_cells)], 1)
    return joined.astype(jnp.bfloat16)

def weights_from_blocks(block_a, block_b, train_count):
    dof_size = block_a.shape[0]
    embedded = jnp.concatenate([jnp.concatenate([block_a, -block_b], 1), jnp.concatenate([block_b, block_a], 1)], 0) / train_count
    loading_level = LOADING * jnp.trace(block_a) / (train_count * dof_size)
    embedded = embedded + loading_level * jnp.eye(2 * dof_size, dtype=jnp.float32)
    factor = jnp.linalg.cholesky(embedded)
    steering = (jnp.arange(2 * dof_size, dtype=jnp.int32)[:, None] // dof_size == jnp.arange(2, dtype=jnp.int32)[None, :]).astype(jnp.float32)
    solved = jax.scipy.linalg.cho_solve((factor, True), steering)
    quiescent = jnp.sum(solved[:dof_size, 0])
    return (solved.T.astype(jnp.bfloat16), quiescent)

def reference(echoes, arc_start, arc_offsets, doppler_bins, steer_angles, train_mask):
    table_re, table_im = doppler_table()

    def per_beam(packed):
        start, offsets, centers, beam_angle, mask_row = packed
        col_index = ((start + offsets) % COLS).astype(jnp.int32)
        beam_cols = jnp.take(echoes, col_index, axis=1)
        snapshots = snapshot(beam_cols, centers, beam_angle, table_re, table_im)
        cell_mask = jnp.repeat(mask_row, BLK).astype(jnp.bfloat16)
        train_count = (BLK * jnp.sum(mask_row)).astype(jnp.float32)

        def per_channel(single):
            gram_sum = jnp.dot((single * cell_mask[None, :]).astype(jnp.float32), single.T.astype(jnp.float32), preferred_element_type=jnp.float32)
            dof_size = gram_sum.shape[0] // 2
            block_a = gram_sum[:dof_size, :dof_size] + gram_sum[dof_size:, dof_size:]
            block_b = gram_sum[dof_size:, :dof_size] - gram_sum[:dof_size, dof_size:]
            adapted, quiescent = weights_from_blocks(block_a, block_b, train_count)
            projected = jnp.dot(adapted.astype(jnp.float32), single.astype(jnp.float32), preferred_element_type=jnp.float32)
            return (projected[0] * projected[0] + projected[1] * projected[1]) / quiescent
        return lax.map(per_channel, snapshots)
    power_map = lax.map(per_beam, (arc_start, arc_offsets, doppler_bins, steer_angles, train_mask))
    padded = jnp.pad(power_map, ((0, 0), (0, 0), (1, 1)))
    row_sums = padded[:, :, :-2] + padded[:, :, 1:-1] + padded[:, :, 2:]
    return (jnp.roll(row_sums, 1, 0) + row_sums + jnp.roll(row_sums, -1, 0)) / 9.0
```

```python
import functools

import jax
import jax.numpy as jnp
from jax import lax
from jax.experimental import pallas as pl
from jax.experimental.pallas import tpu as pltpu
from jax.sharding import PartitionSpec as P

COLS = 256
ARC = 64
BINS = 3
BEAMS = 64
BLK = 128
LOADING = 0.1
VMEM_LIMIT = 48 << 20


def with_halo(block, sides, width, periodic):
    for axis, dim in sides:
        count = lax.axis_size(axis)
        forward = [(i, i + 1) for i in range(count - 1)]
        if periodic:
            forward.append((count - 1, 0))
        backward = [(target, source) for source, target in forward]
        low = lax.ppermute(
            lax.slice_in_dim(block, block.shape[dim] - width, None, axis=dim), axis, forward
        )
        high = lax.ppermute(lax.slice_in_dim(block, 0, width, axis=dim), axis, backward)
        block = jnp.concatenate([low, block, high], axis=dim)
    return block


def doppler_table(num_pulses):
    freq_ids = jnp.arange(num_pulses, dtype=jnp.int32)
    phase_steps = freq_ids[:, None] * freq_ids[None, :] % num_pulses
    phase_angle = -2.0 * jnp.pi / num_pulses * phase_steps.astype(jnp.float32)
    return (jnp.cos(phase_angle).astype(jnp.bfloat16), jnp.sin(phase_angle).astype(jnp.bfloat16))


def snap_gram_kernel(
    col_ref, bins_ref, cos_ref, sin_ref, ext_ref, table_ref, mask_ref, v_ref, gram_ref
):
    beam = pl.program_id(0)
    pulses = ext_ref.shape[2]
    cells = ext_ref.shape[3]
    num_sel = col_ref.shape[1]
    num_chan = bins_ref.shape[1]
    table = table_ref[...]
    parts_re, parts_im = [], []
    for j in range(num_sel):
        col = col_ref[beam, j]
        data = jnp.concatenate([ext_ref[0, col], ext_ref[1, col]], axis=0)
        spec = jnp.dot(table, data, preferred_element_type=jnp.float32)
        cosine = cos_ref[beam, j]
        sine = sin_ref[beam, j]
        spec_re = spec[:pulses]
        spec_im = spec[pulses:]
        parts_re.append(cosine * spec_re - sine * spec_im)
        parts_im.append(sine * spec_re + cosine * spec_im)
    for part, pieces in enumerate((parts_re, parts_im)):
        stacked = jnp.swapaxes(jnp.stack(pieces, 0), 0, 1)
        v_ref[0, part] = stacked.astype(jnp.bfloat16)
    dof = BINS * num_sel
    mask_row = mask_ref[0]
    row = lax.broadcasted_iota(jnp.int32, (dof, dof), 0)
    colm = lax.broadcasted_iota(jnp.int32, (dof, dof), 1)
    lower = row >= colm
    packed = []
    for k in range(num_chan):
        centre = bins_ref[beam, k]
        ids = [(centre + (q - BINS // 2 + pulses)) % pulses for q in range(BINS)]
        u_re = jnp.concatenate([v_ref[0, 0, f] for f in ids], 0)
        u_im = jnp.concatenate([v_ref[0, 1, f] for f in ids], 0)
        right = jnp.concatenate([u_re, u_im], 1)
        m_re = u_re * mask_row
        m_im = u_im * mask_row
        left = jnp.concatenate(
            [jnp.concatenate([m_re, m_im], 1), jnp.concatenate([m_im, -m_re], 1)], 0
        )
        both = lax.dot_general(
            left, right, (((1,), (1,)), ((), ())), preferred_element_type=jnp.float32
        )
        packed.append(jnp.where(lower, both[:dof], both[dof:]))
    gram_ref[0] = jnp.concatenate(packed, 1)


def solve_kernel(hr_in, hi_in, out_ref, hr, hi, xr, xi):
    dof = hr_in.shape[0]
    lanes = hr_in.shape[2]
    nb = dof // 8
    hr[:, :dof, :] = hr_in[...]
    hi[:, :dof, :] = hi_in[...]
    hr[:, dof:, :] = jnp.ones((dof, 8, lanes), jnp.float32)
    hi[:, dof:, :] = jnp.zeros((dof, 8, lanes), jnp.float32)
    xr[...] = jnp.zeros_like(xr)
    xi[...] = jnp.zeros_like(xi)
    trace = jnp.zeros((1, lanes), jnp.float32)
    for i in range(dof):
        trace = trace + hr[i, i : i + 1, :]
    load = (LOADING / dof) * trace
    for i in range(dof):
        hr[i, i : i + 1, :] = hr[i, i : i + 1, :] + load
    sub = lax.broadcasted_iota(jnp.int32, (8, lanes), 0)

    for kb in range(nb):

        def step(k, carry, kb=kb):
            pivot = 1.0 / hr[k, pl.ds(k, 1), :]
            rr = [hr[k, 8 * b : 8 * b + 8, :] for b in range(kb, nb + 1)]
            ri = [hi[k, 8 * b : 8 * b + 8, :] for b in range(kb, nb + 1)]
            for ib in range(kb, nb):
                fr = rr[ib - kb] * pivot
                fi = -ri[ib - kb] * pivot
                if ib == kb:
                    live = sub + 8 * kb > k
                    fr = jnp.where(live, fr, 0.0)
                    fi = jnp.where(live, fi, 0.0)
                for s in range(8):
                    i = 8 * ib + s
                    cr = jnp.broadcast_to(fr[s : s + 1], (8, lanes))
                    ci = jnp.broadcast_to(fi[s : s + 1], (8, lanes))
                    for b in range(ib, nb + 1):
                        pr, pi = rr[b - kb], ri[b - kb]
                        sl = slice(8 * b, 8 * b + 8)
                        hr[i, sl, :] = hr[i, sl, :] - (cr * pr - ci * pi)
                        hi[i, sl, :] = hi[i, sl, :] - (cr * pi + ci * pr)
            return carry

        lax.fori_loop(8 * kb, 8 * kb + 8, step, 0)

    for ib in reversed(range(nb)):

        def back(t, carry, ib=ib):
            i = 8 * ib + 7 - t
            sr = jnp.zeros((8, lanes), jnp.float32)
            si = jnp.zeros((8, lanes), jnp.float32)
            for b in range(ib, nb):
                sl = slice(8 * b, 8 * b + 8)
                ar, ai = hr[i, sl, :], hi[i, sl, :]
                br, bi = xr[sl, :], xi[sl, :]
                sr = sr + (ar * br - ai * bi)
                si = si + (ar * bi + ai * br)
            pivot = 1.0 / hr[i, pl.ds(i, 1), :]
            top_r = hr[i, dof : dof + 1, :]
            top_i = hi[i, dof : dof + 1, :]
            xr[pl.ds(i, 1), :] = (top_r - jnp.sum(sr, 0, keepdims=True)) * pivot
            xi[pl.ds(i, 1), :] = (top_i - jnp.sum(si, 0, keepdims=True)) * pivot
            return carry

        lax.fori_loop(0, 8, back, 0)
    out_ref[:dof, :] = xr[...]
    out_ref[dof : 2 * dof, :] = xi[...]
    out_ref[2 * dof :, :] = jnp.broadcast_to(jnp.sum(xr[...], 0, keepdims=True), (8, lanes))


def power_kernel(w_ref, quiet_ref, v_ref, out_ref):
    num_chan = out_ref.shape[1]
    flat = v_ref[0].reshape(w_ref.shape[2], v_ref.shape[4])
    proj = jnp.dot(w_ref[0], flat, preferred_element_type=jnp.float32)
    p0 = proj[:num_chan]
    p1 = proj[num_chan:]
    out_ref[0] = (p0 * p0 + p1 * p1) / quiet_ref[0]


def body(echoes, arc_start, arc_offsets, doppler_bins, steer_angles, train_mask):
    columns = echoes.shape[1]
    num_pulses = echoes.shape[2]
    cells = echoes.shape[3]
    num_sel = arc_offsets.shape[1]
    chan_count = doppler_bins.shape[1]
    cycle_size = lax.axis_size("az")
    cycle_pos = lax.axis_index("az")
    rng_size = lax.axis_size("rng")
    beam_count = BEAMS // cycle_size
    item_count = beam_count * chan_count
    dof = BINS * num_sel
    table_re, table_im = doppler_table(num_pulses)
    table = jnp.concatenate(
        [jnp.concatenate([table_re, -table_im], 1), jnp.concatenate([table_im, table_re], 1)], 0
    )

    def own(x):
        return lax.dynamic_slice_in_dim(x, cycle_pos * beam_count, beam_count, axis=0)

    extended = with_halo(echoes, (("az", 1),), ARC // 2, True)
    arc_first = (own(arc_start) - cycle_pos * columns + ARC // 2) % COLS
    col_index = arc_first[:, None] + own(arc_offsets)
    bins_own = own(doppler_bins)
    angles = own(steer_angles)
    block_count = train_mask.shape[1]
    cell_mask = (
        jnp.broadcast_to(train_mask[:, :, None], (beam_count, block_count, BLK))
        .reshape(beam_count, 1, block_count * BLK)
        .astype(jnp.bfloat16)
    )
    smem = pl.BlockSpec(memory_space=pltpu.SMEM)
    ext_cols = extended.shape[1]
    v_all, gram = pl.pallas_call(
        snap_gram_kernel,
        grid=(beam_count,),
        in_specs=[
            smem,
            smem,
            smem,
            smem,
            pl.BlockSpec((2, ext_cols, num_pulses, cells), lambda b: (0, 0, 0, 0)),
            pl.BlockSpec(table.shape, lambda b: (0, 0)),
            pl.BlockSpec((1, 1, cells), lambda b: (b, 0, 0)),
        ],
        out_specs=[
            pl.BlockSpec((1, 2, num_pulses, num_sel, cells), lambda b: (b, 0, 0, 0, 0)),
            pl.BlockSpec((1, dof, chan_count * dof), lambda b: (b, 0, 0)),
        ],
        out_shape=[
            jax.ShapeDtypeStruct((beam_count, 2, num_pulses, num_sel, cells), jnp.bfloat16),
            jax.ShapeDtypeStruct((beam_count, dof, chan_count * dof), jnp.float32),
        ],
        compiler_params=pltpu.CompilerParams(vmem_limit_bytes=VMEM_LIMIT),
        name="snap_gram",
    )(col_index, bins_own, jnp.cos(angles), jnp.sin(angles), extended, table, cell_mask)

    per = item_count // rng_size
    if per < chan_count:
        split = chan_count // per
        gram = gram.reshape(beam_count, dof, split, per * dof)
        gram = jnp.swapaxes(gram, 1, 2).reshape(beam_count * split, dof, per * dof)
        width = per
    else:
        width = chan_count
    part = lax.psum_scatter(gram, "rng", scatter_dimension=0, tiled=True)
    lead = part.shape[0]
    mats = part.reshape(lead, dof, width, dof).transpose(1, 3, 0, 2).reshape(dof, dof, per)
    flip = jnp.swapaxes(mats, 0, 1)
    ids = jnp.arange(dof, dtype=jnp.int32)
    row, col = ids[:, None, None], ids[None, :, None]
    h_re = jnp.where(row >= col, mats, flip)
    h_im = jnp.where(row < col, mats, jnp.where(row > col, -flip, 0.0))
    vm = pltpu.VMEM
    solved = pl.pallas_call(
        solve_kernel,
        out_shape=jax.ShapeDtypeStruct((2 * dof + 8, per), jnp.float32),
        scratch_shapes=[
            vm((dof, dof + 8, per), jnp.float32),
            vm((dof, dof + 8, per), jnp.float32),
            vm((dof, per), jnp.float32),
            vm((dof, per), jnp.float32),
        ],
        compiler_params=pltpu.CompilerParams(vmem_limit_bytes=VMEM_LIMIT),
        name="solve",
    )(h_re, h_im)
    body_size = (2 * dof + 1) * per
    local_count = (BLK * jnp.sum(train_mask, axis=1)).astype(jnp.float32)
    payload = jnp.concatenate([solved[: 2 * dof + 1].reshape(body_size), local_count])
    gathered = lax.all_gather(payload, "rng", axis=0)
    count = jnp.sum(gathered[:, body_size:], axis=0)
    sol = gathered[:, :body_size].reshape(rng_size, 2 * dof + 1, per)
    sol = jnp.swapaxes(sol, 1, 2).reshape(beam_count, chan_count, 2 * dof + 1)
    sol = sol * count[:, None, None]
    quiet = sol[:, :, 2 * dof :]
    adapted = sol[:, :, : 2 * dof].astype(jnp.bfloat16)
    adapted = adapted.reshape(beam_count, chan_count, 2, BINS, 1, num_sel)
    freq = jnp.arange(num_pulses, dtype=jnp.int32)
    spread = jnp.zeros((beam_count, chan_count, 2, num_pulses, num_sel), jnp.bfloat16)
    for q in range(BINS):
        hit = ((bins_own + (q - BINS // 2)) % num_pulses)[:, :, None] == freq
        spread = jnp.where(hit[:, :, None, :, None], adapted[:, :, :, q], spread)
    taps = num_pulses * num_sel
    spread = spread.reshape(beam_count, chan_count, 2, taps)
    w_re, w_im = spread[:, :, 0], spread[:, :, 1]
    weights = jnp.concatenate(
        [jnp.concatenate([w_re, w_im], 2), jnp.concatenate([-w_im, w_re], 2)], 1
    )
    power_map = pl.pallas_call(
        power_kernel,
        grid=(beam_count,),
        in_specs=[
            pl.BlockSpec((1, 2 * chan_count, 2 * taps), lambda b: (b, 0, 0)),
            pl.BlockSpec((1, chan_count, 1), lambda b: (b, 0, 0)),
            pl.BlockSpec((1, 2, num_pulses, num_sel, cells), lambda b: (b, 0, 0, 0, 0)),
        ],
        out_specs=pl.BlockSpec((1, chan_count, cells), lambda b: (b, 0, 0)),
        out_shape=jax.ShapeDtypeStruct((beam_count, chan_count, cells), jnp.float32),
        compiler_params=pltpu.CompilerParams(vmem_limit_bytes=VMEM_LIMIT),
        name="power",
    )(weights, quiet, v_all)
    range_ext = with_halo(power_map, (("rng", 2),), 1, False)
    row_sums = range_ext[:, :, :-2] + range_ext[:, :, 1:-1] + range_ext[:, :, 2:]
    beam_ext = with_halo(row_sums, (("az", 0),), 1, True)
    return (beam_ext[:-2] + beam_ext[1:-1] + beam_ext[2:]) / 9.0


def solution(mesh):
    return jax.shard_map(
        body,
        mesh=mesh,
        in_specs=(P(None, "az", None, "rng"), P(), P(), P(), P(), P("az", "rng")),
        out_specs=P("az", None, "rng"),
        check_vma=False,
    )
```

```python
import functools

import jax
import jax.numpy as jnp
from jax import lax
from jax.experimental import pallas as pl
from jax.experimental.pallas import tpu as pltpu
from jax.sharding import PartitionSpec as P

COLS = 256
ARC = 64
BINS = 3
BEAMS = 64
BLK = 128
LOADING = 0.1
VMEM_LIMIT = 48 << 20


def doppler_table(num_pulses):
    freq_ids = jnp.arange(num_pulses, dtype=jnp.int32)
    phase_steps = freq_ids[:, None] * freq_ids[None, :] % num_pulses
    phase_angle = -2.0 * jnp.pi / num_pulses * phase_steps.astype(jnp.float32)
    return (jnp.cos(phase_angle).astype(jnp.bfloat16), jnp.sin(phase_angle).astype(jnp.bfloat16))


def snap_gram_kernel(
    col_ref, bins_ref, cos_ref, sin_ref, ext_ref, table_ref, mask_ref, v_ref, gram_ref
):
    beam = pl.program_id(0)
    pulses = ext_ref.shape[2]
    cells = ext_ref.shape[3]
    num_sel = col_ref.shape[1]
    num_chan = bins_ref.shape[1]
    table = table_ref[...]
    parts_re, parts_im = [], []
    for j in range(num_sel):
        col = col_ref[beam, j]
        data = jnp.concatenate([ext_ref[0, col], ext_ref[1, col]], axis=0)
        spec = jnp.dot(table, data, preferred_element_type=jnp.float32)
        cosine = cos_ref[beam, j]
        sine = sin_ref[beam, j]
        spec_re = spec[:pulses]
        spec_im = spec[pulses:]
        parts_re.append(cosine * spec_re - sine * spec_im)
        parts_im.append(sine * spec_re + cosine * spec_im)
    for part, pieces in enumerate((parts_re, parts_im)):
        stacked = jnp.swapaxes(jnp.stack(pieces, 0), 0, 1)
        v_ref[0, part] = stacked.astype(jnp.bfloat16)
    dof = BINS * num_sel
    mask_row = mask_ref[0]
    row = lax.broadcasted_iota(jnp.int32, (dof, dof), 0)
    colm = lax.broadcasted_iota(jnp.int32, (dof, dof), 1)
    lower = row >= colm
    packed = []
    for k in range(num_chan):
        centre = bins_ref[beam, k]
        ids = [(centre + (q - BINS // 2 + pulses)) % pulses for q in range(BINS)]
        u_re = jnp.concatenate([v_ref[0, 0, f] for f in ids], 0)
        u_im = jnp.concatenate([v_ref[0, 1, f] for f in ids], 0)
        right = jnp.concatenate([u_re, u_im], 1)
        m_re = u_re * mask_row
        m_im = u_im * mask_row
        left = jnp.concatenate(
            [jnp.concatenate([m_re, m_im], 1), jnp.concatenate([m_im, -m_re], 1)], 0
        )
        both = lax.dot_general(
            left, right, (((1,), (1,)), ((), ())), preferred_element_type=jnp.float32
        )
        packed.append(jnp.where(lower, both[:dof], both[dof:]))
    gram_ref[0] = jnp.concatenate(packed, 1)


def solve_kernel(hr_in, hi_in, out_ref, hr, hi, xr, xi):
    dof = hr_in.shape[0]
    lanes = hr_in.shape[2]
    nb = dof // 8
    hr[:, :dof, :] = hr_in[...]
    hi[:, :dof, :] = hi_in[...]
    hr[:, dof:, :] = jnp.ones((dof, 8, lanes), jnp.float32)
    hi[:, dof:, :] = jnp.zeros((dof, 8, lanes), jnp.float32)
    xr[...] = jnp.zeros_like(xr)
    xi[...] = jnp.zeros_like(xi)
    trace = jnp.zeros((1, lanes), jnp.float32)
    for i in range(dof):
        trace = trace + hr[i, i : i + 1, :]
    load = (LOADING / dof) * trace
    for i in range(dof):
        hr[i, i : i + 1, :] = hr[i, i : i + 1, :] + load
    sub = lax.broadcasted_iota(jnp.int32, (8, lanes), 0)

    for kb in range(nb):

        def step(k, carry, kb=kb):
            pivot = 1.0 / hr[k, pl.ds(k, 1), :]
            rr = [hr[k, 8 * b : 8 * b + 8, :] for b in range(kb, nb + 1)]
            ri = [hi[k, 8 * b : 8 * b + 8, :] for b in range(kb, nb + 1)]
            for ib in range(kb, nb):
                fr = rr[ib - kb] * pivot
                fi = -ri[ib - kb] * pivot
                if ib == kb:
                    live = sub + 8 * kb > k
                    fr = jnp.where(live, fr, 0.0)
                    fi = jnp.where(live, fi, 0.0)
                for s in range(8):
                    i = 8 * ib + s
                    cr = jnp.broadcast_to(fr[s : s + 1], (8, lanes))
                    ci = jnp.broadcast_to(fi[s : s + 1], (8, lanes))
                    for b in range(ib, nb + 1):
                        pr, pi = rr[b - kb], ri[b - kb]
                        sl = slice(8 * b, 8 * b + 8)
                        hr[i, sl, :] = hr[i, sl, :] - (cr * pr - ci * pi)
                        hi[i, sl, :] = hi[i, sl, :] - (cr * pi + ci * pr)
            return carry

        lax.fori_loop(8 * kb, 8 * kb + 8, step, 0)

    for ib in reversed(range(nb)):

        def back(t, carry, ib=ib):
            i = 8 * ib + 7 - t
            sr = jnp.zeros((8, lanes), jnp.float32)
            si = jnp.zeros((8, lanes), jnp.float32)
            for b in range(ib, nb):
                sl = slice(8 * b, 8 * b + 8)
                ar, ai = hr[i, sl, :], hi[i, sl, :]
                br, bi = xr[sl, :], xi[sl, :]
                sr = sr + (ar * br - ai * bi)
                si = si + (ar * bi + ai * br)
            pivot = 1.0 / hr[i, pl.ds(i, 1), :]
            top_r = hr[i, dof : dof + 1, :]
            top_i = hi[i, dof : dof + 1, :]
            xr[pl.ds(i, 1), :] = (top_r - jnp.sum(sr, 0, keepdims=True)) * pivot
            xi[pl.ds(i, 1), :] = (top_i - jnp.sum(si, 0, keepdims=True)) * pivot
            return carry

        lax.fori_loop(0, 8, back, 0)
    out_ref[:dof, :] = xr[...]
    out_ref[dof : 2 * dof, :] = xi[...]
    out_ref[2 * dof :, :] = jnp.broadcast_to(jnp.sum(xr[...], 0, keepdims=True), (8, lanes))


MESH = pl.DeviceIdType.MESH


def scatter_kernel(n, g_ref, out_ref, pair, acc, right, left, psend, precv, rsend, rrecv, lsend, lrecv):
    me = lax.axis_index("rng")
    z = me // 2
    c = me % 2
    mate = 2 * z + 1 - c
    ahead = lax.rem(me + 2, 2 * n)
    behind = lax.rem(me + 2 * n - 2, 2 * n)
    barrier = pltpu.get_barrier_semaphore()
    pl.semaphore_signal(barrier, inc=1, device_id={"rng": mate}, device_id_type=MESH)
    pl.semaphore_signal(barrier, inc=1, device_id={"rng": ahead}, device_id_type=MESH)
    pl.semaphore_signal(barrier, inc=1, device_id={"rng": behind}, device_id_type=MESH)
    pl.semaphore_wait(barrier, 3)

    order = []
    for t in range((n + 1) // 2):
        order.append(n - 1 - t)
        if t != n - 1 - t:
            order.append(t)

    def pair_copy(t):
        return pltpu.make_async_remote_copy(
            src_ref=g_ref.at[2 * t + 1 - c],
            dst_ref=pair.at[t],
            send_sem=psend.at[t],
            recv_sem=precv.at[t],
            device_id={"rng": mate},
            device_id_type=MESH,
        )

    def right_copy(t):
        return pltpu.make_async_remote_copy(
            src_ref=acc.at[t],
            dst_ref=right.at[t],
            send_sem=rsend.at[t],
            recv_sem=rrecv.at[t],
            device_id={"rng": ahead},
            device_id_type=MESH,
        )

    def left_copy(t):
        return pltpu.make_async_remote_copy(
            src_ref=acc.at[t],
            dst_ref=left.at[t],
            send_sem=lsend.at[t],
            recv_sem=lrecv.at[t],
            device_id={"rng": behind},
            device_id_type=MESH,
        )

    for t in order:
        pair_copy(t).start()
    for t in order:
        pair_copy(t).wait_recv()
        acc[t] = g_ref[2 * t + c] + pair[t]

        @pl.when(jnp.logical_and(z == 0, t > 0))
        def _(t=t):
            right_copy(t).start()

        @pl.when(jnp.logical_and(z == n - 1, t < n - 1))
        def _(t=t):
            left_copy(t).start()

    for s in range(n - 1):
        t = n - 1 - s

        @pl.when(jnp.logical_and(z > 0, z < t))
        def _(t=t):
            right_copy(t).wait_recv()
            acc[t] = acc[t] + right[t]
            right_copy(t).start()

        @pl.when(jnp.logical_and(z < n - 1, z > s))
        def _(t=s):
            left_copy(t).wait_recv()
            acc[t] = acc[t] + left[t]
            left_copy(t).start()

    for t in range(n):

        @pl.when(z == t)
        def _(t=t):
            total = acc[t]
            if t > 0:
                right_copy(t).wait_recv()
                total = total + right[t]
            if t < n - 1:
                left_copy(t).wait_recv()
                total = total + left[t]
            out_ref[...] = total

    for t in range(n):
        pair_copy(t).wait_send()

        @pl.when(z < t)
        def _(t=t):
            right_copy(t).wait_send()

        @pl.when(z > t)
        def _(t=t):
            left_copy(t).wait_send()


def apply_kernel(
    halves,
    per,
    dof,
    pay_ref,
    bins_ref,
    *refs,
):
    v_refs = refs[:halves]
    (out_ref, v_all, gat, expand, power, edge, halo, sums, az_lo, az_hi) = refs[halves : halves + 10]
    (vsem, gsend, grecv, esend, erecv, asend, arecv) = refs[halves + 10 :]
    me = lax.axis_index("rng")
    az = lax.axis_index("az")
    n = lax.axis_size("rng")
    m = lax.axis_size("az")
    beams, num_chan, cells = out_ref.shape
    pulses, num_sel = v_all.shape[2], v_all.shape[3]
    taps = pulses * num_sel
    az_next = lax.rem(az + 1, m)
    az_prev = lax.rem(az + m - 1, m)
    barrier = pltpu.get_barrier_semaphore()
    for d in range(1, n):
        peer = lax.rem(me + d, n)
        pl.semaphore_signal(barrier, inc=1, device_id={"rng": peer}, device_id_type=MESH)
    for other in (az_next, az_prev):
        pl.semaphore_signal(barrier, inc=1, device_id={"az": other}, device_id_type=MESH)
    share = beams // halves
    loads = []
    for h in range(halves):
        load = pltpu.make_async_copy(v_refs[h], v_all.at[pl.ds(h * share, share)], vsem.at[h])
        load.start()
        loads.append(load)
    pl.semaphore_wait(barrier, n + 1)

    copies = []
    for d in range(1, n):
        peer = lax.rem(me + d, n)
        copy = pltpu.make_async_remote_copy(
            src_ref=pay_ref,
            dst_ref=gat.at[me],
            send_sem=gsend.at[d],
            recv_sem=grecv.at[d],
            device_id={"rng": peer},
            device_id_type=MESH,
        )
        copy.start()
        copies.append(copy)
    gat[me] = pay_ref[...]
    depth = expand.shape[1]
    wide = expand.shape[2]
    src = lax.broadcasted_iota(jnp.int32, (depth, wide), 0)
    dst = lax.broadcasted_iota(jnp.int32, (depth, wide), 1)
    want = (dst // taps) * num_sel + dst % num_sel
    expand[0] = (src == want).astype(jnp.float32).astype(jnp.bfloat16)
    expand[1] = (src == want + dof).astype(jnp.float32).astype(jnp.bfloat16)
    for load in loads:
        load.wait()
    for copy in copies:
        copy.wait_recv()
    rows = gat.shape[1] - beams
    count = jnp.zeros((beams, gat.shape[2]), jnp.float32)
    for r in range(n):
        count = count + gat[r, rows:, :]
    sums[0] = jnp.zeros(sums.shape[1:], jnp.float32)
    for b in range(beams):
        sums[b, :1, :] = count[b : b + 1]
    freq = lax.broadcasted_iota(jnp.int32, (num_chan, taps), 1) // num_sel

    def one(b, carry):
        if per >= num_chan:
            ratio = per // num_chan
            start = pl.multiple_of((b % ratio) * num_chan, 8)
            w = gat[b // ratio, pl.ds(start, num_chan), :]
        else:
            split = num_chan // per
            w = jnp.concatenate([gat[b * split + t, :per, :] for t in range(split)], 0)
        w = w * sums[b, :1, :]
        quiet = w[:, 2 * dof : 2 * dof + 1]
        wb = w.astype(jnp.bfloat16)
        centre = bins_ref[b]
        planes = []
        for part in range(2):
            spread = jnp.dot(wb, expand[part], preferred_element_type=jnp.float32)
            plane = jnp.zeros((num_chan, taps), jnp.float32)
            for q in range(BINS):
                f = lax.rem(centre + (q - BINS // 2 + pulses), pulses)
                plane = jnp.where(freq == f, spread[:, q * taps : (q + 1) * taps], plane)
            planes.append(plane)
        top = jnp.concatenate([planes[0], planes[1]], 1)
        low = jnp.concatenate([-planes[1], planes[0]], 1)
        lhs = jnp.concatenate([top, low], 0).astype(jnp.bfloat16)
        flat = v_all[b].reshape(2 * taps, cells)
        proj = jnp.dot(lhs, flat, preferred_element_type=jnp.float32)
        p0 = proj[:num_chan]
        p1 = proj[num_chan:]
        power[b] = (p0 * p0 + p1 * p1) / quiet
        return carry

    lax.fori_loop(0, beams, one, 0)
    items = beams * num_chan
    turned = power[...].reshape(items, cells).T
    edge[0] = turned[:8]
    edge[1] = turned[cells - 8 :]

    def edge_copy(side):
        target = lax.rem(me + 1, n) if side else lax.rem(me + n - 1, n)
        return pltpu.make_async_remote_copy(
            src_ref=edge.at[side],
            dst_ref=halo.at[side],
            send_sem=esend.at[side],
            recv_sem=erecv.at[side],
            device_id={"rng": target},
            device_id_type=MESH,
        )

    for side in range(2):
        edge_copy(side).start()
    for side in range(2):
        edge_copy(side).wait()
    before = jnp.where(me > 0, halo[1, 7:8], 0.0)
    after = jnp.where(me < n - 1, halo[0, 0:1], 0.0)
    turned = (
        jnp.concatenate([before, turned[:-1]], 0)
        + turned
        + jnp.concatenate([turned[1:], after], 0)
    )
    sums[...] = turned.T.reshape(beams, num_chan, cells)
    up = pltpu.make_async_remote_copy(
        src_ref=sums.at[beams - 1],
        dst_ref=az_lo,
        send_sem=asend.at[0],
        recv_sem=arecv.at[0],
        device_id={"az": az_next},
        device_id_type=MESH,
    )
    down = pltpu.make_async_remote_copy(
        src_ref=sums.at[0],
        dst_ref=az_hi,
        send_sem=asend.at[1],
        recv_sem=arecv.at[1],
        device_id={"az": az_prev},
        device_id_type=MESH,
    )
    up.start()
    down.start()
    for b in range(1, beams - 1):
        out_ref[b] = (sums[b - 1] + sums[b] + sums[b + 1]) / 9.0
    up.wait_recv()
    down.wait_recv()
    out_ref[0] = (az_lo[...] + sums[0] + sums[1]) / 9.0
    out_ref[beams - 1] = (sums[beams - 2] + sums[beams - 1] + az_hi[...]) / 9.0
    up.wait_send()
    down.wait_send()
    for copy in copies:
        copy.wait_send()


def body(echoes, arc_start, arc_offsets, doppler_bins, steer_angles, train_mask):
    columns = echoes.shape[1]
    num_pulses = echoes.shape[2]
    cells = echoes.shape[3]
    num_sel = arc_offsets.shape[1]
    chan_count = doppler_bins.shape[1]
    cycle_size = lax.axis_size("az")
    cycle_pos = lax.axis_index("az")
    rng_size = lax.axis_size("rng")
    beam_count = BEAMS // cycle_size
    item_count = beam_count * chan_count
    dof = BINS * num_sel
    table_re, table_im = doppler_table(num_pulses)
    table = jnp.concatenate(
        [jnp.concatenate([table_re, -table_im], 1), jnp.concatenate([table_im, table_re], 1)], 0
    )

    def own(x):
        return lax.dynamic_slice_in_dim(x, cycle_pos * beam_count, beam_count, axis=0)

    arc_first = (own(arc_start) - cycle_pos * columns + ARC // 2) % COLS
    col_index = arc_first[:, None] + own(arc_offsets)
    bins_own = own(doppler_bins)
    angles = own(steer_angles)
    block_count = train_mask.shape[1]
    cell_mask = (
        jnp.broadcast_to(train_mask[:, :, None], (beam_count, block_count, BLK))
        .reshape(beam_count, 1, block_count * BLK)
        .astype(jnp.bfloat16)
    )
    smem = pl.BlockSpec(memory_space=pltpu.SMEM)

    def snap_gram(extended, first, last, base):
        share = last - first
        ext_cols = extended.shape[1]
        return pl.pallas_call(
            snap_gram_kernel,
            grid=(share,),
            in_specs=[
                smem,
                smem,
                smem,
                smem,
                pl.BlockSpec((2, ext_cols, num_pulses, cells), lambda b: (0, 0, 0, 0)),
                pl.BlockSpec(table.shape, lambda b: (0, 0)),
                pl.BlockSpec((1, 1, cells), lambda b: (b, 0, 0)),
            ],
            out_specs=[
                pl.BlockSpec((1, 2, num_pulses, num_sel, cells), lambda b: (b, 0, 0, 0, 0)),
                pl.BlockSpec((1, dof, chan_count * dof), lambda b: (b, 0, 0)),
            ],
            out_shape=[
                jax.ShapeDtypeStruct((share, 2, num_pulses, num_sel, cells), jnp.bfloat16),
                jax.ShapeDtypeStruct((share, dof, chan_count * dof), jnp.float32),
            ],
            compiler_params=pltpu.CompilerParams(vmem_limit_bytes=VMEM_LIMIT),
            cost_estimate=pl.CostEstimate(
                flops=share * 600_000_000, bytes_accessed=share * 1_500_000, transcendentals=0
            ),
            name="snap_gram",
        )(
            col_index[first:last] - base,
            bins_own[first:last],
            jnp.cos(angles)[first:last],
            jnp.sin(angles)[first:last],
            extended,
            table,
            cell_mask[first:last],
        )

    width = ARC // 2
    forward = [(i, (i + 1) % cycle_size) for i in range(cycle_size)]
    backward = [(target, source) for source, target in forward]
    low = lax.ppermute(echoes[:, columns - width :], "az", forward)
    high = lax.ppermute(echoes[:, :width], "az", backward)
    step = COLS // BEAMS
    half = beam_count // 2
    if (half - 1) * step + step - 1 + ARC - 1 < width + columns and half * step >= width:
        v_lo, gram_lo = snap_gram(jnp.concatenate([low, echoes], 1), 0, half, 0)
        v_hi, gram_hi = snap_gram(jnp.concatenate([echoes, high], 1), half, beam_count, width)
        v_parts = (v_lo, v_hi)
        gram = jnp.concatenate([gram_lo, gram_hi], 0)
    else:
        v_one, gram = snap_gram(jnp.concatenate([low, echoes, high], 1), 0, beam_count, 0)
        v_parts = (v_one,)

    per = item_count // rng_size
    if per < chan_count:
        split = chan_count // per
        gram = gram.reshape(beam_count, dof, split, per * dof)
        gram = jnp.swapaxes(gram, 1, 2).reshape(beam_count * split, dof, per * dof)
        width = per
    else:
        width = chan_count
    vm = pltpu.VMEM
    dma = pltpu.SemaphoreType.DMA
    line = rng_size // 2
    chunk = (gram.shape[0] // rng_size, dof, gram.shape[2])
    part = pl.pallas_call(
        functools.partial(scatter_kernel, line),
        in_specs=[pl.BlockSpec(memory_space=vm)],
        out_specs=pl.BlockSpec(memory_space=vm),
        out_shape=jax.ShapeDtypeStruct(chunk, jnp.float32),
        scratch_shapes=[vm((line,) + chunk, jnp.float32)] * 4 + [dma((line,))] * 6,
        compiler_params=pltpu.CompilerParams(
            collective_id=0, has_side_effects=True, vmem_limit_bytes=VMEM_LIMIT
        ),
        name="scatter",
    )(gram.reshape((rng_size,) + chunk))
    lead = part.shape[0]
    mats = part.reshape(lead, dof, width, dof).transpose(1, 3, 0, 2).reshape(dof, dof, per)
    flip = jnp.swapaxes(mats, 0, 1)
    ids = jnp.arange(dof, dtype=jnp.int32)
    row, col = ids[:, None, None], ids[None, :, None]
    h_re = jnp.where(row >= col, mats, flip)
    h_im = jnp.where(row < col, mats, jnp.where(row > col, -flip, 0.0))
    solved = pl.pallas_call(
        solve_kernel,
        out_shape=jax.ShapeDtypeStruct((2 * dof + 8, per), jnp.float32),
        scratch_shapes=[
            vm((dof, dof + 8, per), jnp.float32),
            vm((dof, dof + 8, per), jnp.float32),
            vm((dof, per), jnp.float32),
            vm((dof, per), jnp.float32),
        ],
        compiler_params=pltpu.CompilerParams(vmem_limit_bytes=VMEM_LIMIT),
        name="solve",
    )(h_re, h_im)
    lanes = 128
    local_count = (BLK * jnp.sum(train_mask, axis=1)).astype(jnp.float32)
    pad_rows = -per % 8
    payload = jnp.concatenate(
        [
            jnp.pad(solved.T, ((0, pad_rows), (0, lanes - solved.shape[0]))),
            jnp.broadcast_to(local_count[:, None], (beam_count, lanes)),
        ],
        0,
    )
    halves = len(v_parts)
    any_spec = pl.BlockSpec(memory_space=pl.ANY)
    taps = num_pulses * num_sel
    block = (chan_count, cells)
    out = pl.pallas_call(
        functools.partial(apply_kernel, halves, per, dof),
        in_specs=[pl.BlockSpec(memory_space=vm)] * 2 + [any_spec] * halves,
        out_specs=pl.BlockSpec(memory_space=vm),
        out_shape=jax.ShapeDtypeStruct((beam_count,) + block, jnp.float32),
        scratch_shapes=[
            vm((beam_count, 2, num_pulses, num_sel, cells), jnp.bfloat16),
            vm((rng_size,) + payload.shape, jnp.float32),
            vm((2, lanes, BINS * taps), jnp.bfloat16),
            vm((beam_count,) + block, jnp.float32),
            vm((2, 8, item_count), jnp.float32),
            vm((2, 8, item_count), jnp.float32),
            vm((beam_count,) + block, jnp.float32),
            vm(block, jnp.float32),
            vm(block, jnp.float32),
            dma((halves,)),
            dma((rng_size,)),
            dma((rng_size,)),
            dma((2,)),
            dma((2,)),
            dma((2,)),
            dma((2,)),
        ],
        compiler_params=pltpu.CompilerParams(
            collective_id=1, has_side_effects=True, vmem_limit_bytes=VMEM_LIMIT
        ),
        name="apply",
    )(payload, bins_own[:, :, None], *v_parts)
    return out


def solution(mesh):
    return jax.shard_map(
        body,
        mesh=mesh,
        in_specs=(P(None, "az", None, "rng"), P(), P(), P(), P(), P("az", "rng")),
        out_specs=P("az", None, "rng"),
        check_vma=False,
    )
```

```python
import functools

import jax
import jax.numpy as jnp
from jax import lax
from jax.experimental import pallas as pl
from jax.experimental.pallas import tpu as pltpu
from jax.sharding import PartitionSpec as P


COLS = 256
ARC = 64
BINS = 3
BEAMS = 64
BLK = 128
LOADING = 0.1
VMEM_LIMIT = 48 << 20


def doppler_table(num_pulses):
    freq_ids = jnp.arange(num_pulses, dtype=jnp.int32)
    phase_steps = freq_ids[:, None] * freq_ids[None, :] % num_pulses
    phase_angle = -2.0 * jnp.pi / num_pulses * phase_steps.astype(jnp.float32)
    return (jnp.cos(phase_angle).astype(jnp.bfloat16), jnp.sin(phase_angle).astype(jnp.bfloat16))


def snap_gram_kernel(
    col_ref, bins_ref, cos_ref, sin_ref, ext_ref, table_ref, mask_ref, v_ref, gram_ref
):
    beam = pl.program_id(0)
    pulses = ext_ref.shape[2]
    num_sel = col_ref.shape[1]
    num_chan = bins_ref.shape[1]
    table = table_ref[...]
    parts_re, parts_im = [], []
    for j in range(num_sel):
        col = col_ref[beam, j]
        data = jnp.concatenate([ext_ref[0, col], ext_ref[1, col]], axis=0)
        spec = jnp.dot(table, data, preferred_element_type=jnp.float32)
        cosine = cos_ref[beam, j]
        sine = sin_ref[beam, j]
        spec_re = spec[:pulses]
        spec_im = spec[pulses:]
        parts_re.append(cosine * spec_re - sine * spec_im)
        parts_im.append(sine * spec_re + cosine * spec_im)
    for part, pieces in enumerate((parts_re, parts_im)):
        stacked = jnp.swapaxes(jnp.stack(pieces, 0), 0, 1)
        v_ref[0, part] = stacked.astype(jnp.bfloat16)
    dof = BINS * num_sel
    mask_row = mask_ref[0]
    row = lax.broadcasted_iota(jnp.int32, (dof, dof), 0)
    colm = lax.broadcasted_iota(jnp.int32, (dof, dof), 1)
    lower = row >= colm
    packed = []
    for k in range(num_chan):
        centre = bins_ref[beam, k]
        ids = [(centre + (q - BINS // 2 + pulses)) % pulses for q in range(BINS)]
        u_re = jnp.concatenate([v_ref[0, 0, f] for f in ids], 0)
        u_im = jnp.concatenate([v_ref[0, 1, f] for f in ids], 0)
        right = jnp.concatenate([u_re, u_im], 1)
        m_re = u_re * mask_row
        m_im = u_im * mask_row
        left = jnp.concatenate(
            [jnp.concatenate([m_re, m_im], 1), jnp.concatenate([m_im, -m_re], 1)], 0
        )
        both = lax.dot_general(
            left, right, (((1,), (1,)), ((), ())), preferred_element_type=jnp.float32
        )
        packed.append(jnp.where(lower, both[:dof], both[dof:]))
    gram_ref[0] = jnp.concatenate(packed, 1)


def solve_kernel(hr_in, hi_in, out_ref, hr, hi, xr, xi):
    dof = hr_in.shape[0]
    lanes = hr_in.shape[2]
    nb = dof // 8
    hr[:, :dof, :] = hr_in[...]
    hi[:, :dof, :] = hi_in[...]
    hr[:, dof:, :] = jnp.ones((dof, 8, lanes), jnp.float32)
    hi[:, dof:, :] = jnp.zeros((dof, 8, lanes), jnp.float32)
    xr[...] = jnp.zeros_like(xr)
    xi[...] = jnp.zeros_like(xi)
    trace = jnp.zeros((1, lanes), jnp.float32)
    for i in range(dof):
        trace = trace + hr[i, i : i + 1, :]
    load = (LOADING / dof) * trace
    for i in range(dof):
        hr[i, i : i + 1, :] = hr[i, i : i + 1, :] + load
    sub = lax.broadcasted_iota(jnp.int32, (8, lanes), 0)

    for kb in range(nb):

        def step(k, carry, kb=kb):
            pivot = 1.0 / hr[k, pl.ds(k, 1), :]
            rr = [hr[k, 8 * b : 8 * b + 8, :] for b in range(kb, nb + 1)]
            ri = [hi[k, 8 * b : 8 * b + 8, :] for b in range(kb, nb + 1)]
            for ib in range(kb, nb):
                fr = rr[ib - kb] * pivot
                fi = -ri[ib - kb] * pivot
                if ib == kb:
                    live = sub + 8 * kb > k
                    fr = jnp.where(live, fr, 0.0)
                    fi = jnp.where(live, fi, 0.0)
                for s in range(8):
                    i = 8 * ib + s
                    cr = jnp.broadcast_to(fr[s : s + 1], (8, lanes))
                    ci = jnp.broadcast_to(fi[s : s + 1], (8, lanes))
                    for b in range(ib, nb + 1):
                        pr, pi = rr[b - kb], ri[b - kb]
                        sl = slice(8 * b, 8 * b + 8)
                        hr[i, sl, :] = hr[i, sl, :] - (cr * pr - ci * pi)
                        hi[i, sl, :] = hi[i, sl, :] - (cr * pi + ci * pr)
            return carry

        lax.fori_loop(8 * kb, 8 * kb + 8, step, 0)

    for ib in reversed(range(nb)):

        def back(t, carry, ib=ib):
            i = 8 * ib + 7 - t
            sr = jnp.zeros((8, lanes), jnp.float32)
            si = jnp.zeros((8, lanes), jnp.float32)
            for b in range(ib, nb):
                sl = slice(8 * b, 8 * b + 8)
                ar, ai = hr[i, sl, :], hi[i, sl, :]
                br, bi = xr[sl, :], xi[sl, :]
                sr = sr + (ar * br - ai * bi)
                si = si + (ar * bi + ai * br)
            pivot = 1.0 / hr[i, pl.ds(i, 1), :]
            top_r = hr[i, dof : dof + 1, :]
            top_i = hi[i, dof : dof + 1, :]
            xr[pl.ds(i, 1), :] = (top_r - jnp.sum(sr, 0, keepdims=True)) * pivot
            xi[pl.ds(i, 1), :] = (top_i - jnp.sum(si, 0, keepdims=True)) * pivot
            return carry

        lax.fori_loop(0, 8, back, 0)
    out_ref[:dof, :] = xr[...]
    out_ref[dof : 2 * dof, :] = xi[...]
    out_ref[2 * dof :, :] = jnp.broadcast_to(jnp.sum(xr[...], 0, keepdims=True), (8, lanes))


MESH = pl.DeviceIdType.MESH


def scatter_kernel(n, g_ref, out_ref, pair, acc, right, left, psend, precv, rsend, rrecv, lsend, lrecv):
    me = lax.axis_index("rng")
    z = me // 2
    c = me % 2
    mate = 2 * z + 1 - c
    ahead = lax.rem(me + 2, 2 * n)
    behind = lax.rem(me + 2 * n - 2, 2 * n)
    barrier = pltpu.get_barrier_semaphore()
    pl.semaphore_signal(barrier, inc=1, device_id={"rng": mate}, device_id_type=MESH)
    pl.semaphore_signal(barrier, inc=1, device_id={"rng": ahead}, device_id_type=MESH)
    pl.semaphore_signal(barrier, inc=1, device_id={"rng": behind}, device_id_type=MESH)
    pl.semaphore_wait(barrier, 3)

    order = []
    for t in range((n + 1) // 2):
        order.append(n - 1 - t)
        if t != n - 1 - t:
            order.append(t)

    def pair_copy(t):
        return pltpu.make_async_remote_copy(
            src_ref=g_ref.at[2 * t + 1 - c],
            dst_ref=pair.at[t],
            send_sem=psend.at[t],
            recv_sem=precv.at[t],
            device_id={"rng": mate},
            device_id_type=MESH,
        )

    def right_copy(t):
        return pltpu.make_async_remote_copy(
            src_ref=acc.at[t],
            dst_ref=right.at[t],
            send_sem=rsend.at[t],
            recv_sem=rrecv.at[t],
            device_id={"rng": ahead},
            device_id_type=MESH,
        )

    def left_copy(t):
        return pltpu.make_async_remote_copy(
            src_ref=acc.at[t],
            dst_ref=left.at[t],
            send_sem=lsend.at[t],
            recv_sem=lrecv.at[t],
            device_id={"rng": behind},
            device_id_type=MESH,
        )

    for t in order:
        pair_copy(t).start()
    for t in order:
        pair_copy(t).wait_recv()
        acc[t] = g_ref[2 * t + c] + pair[t]

        @pl.when(jnp.logical_and(z == 0, t > 0))
        def _(t=t):
            right_copy(t).start()

        @pl.when(jnp.logical_and(z == n - 1, t < n - 1))
        def _(t=t):
            left_copy(t).start()

    for place in range(n):
        events = [(place + n - 1 - t, 0, t) for t in range(place + 1, n) if place > 0]
        events += [(n - 1 - place + t, 1, t) for t in range(place) if place < n - 1]

        @pl.when(z == place)
        def _(place=place, events=sorted(events)):
            for _, side, t in events:
                copy = left_copy(t) if side else right_copy(t)
                source = left if side else right
                copy.wait_recv()
                acc[t] = acc[t] + source[t]
                copy.start()
            total = acc[place]
            if place > 0:
                right_copy(place).wait_recv()
                total = total + right[place]
            if place < n - 1:
                left_copy(place).wait_recv()
                total = total + left[place]
            out_ref[...] = total

    for t in range(n):
        pair_copy(t).wait_send()

        @pl.when(z < t)
        def _(t=t):
            right_copy(t).wait_send()

        @pl.when(z > t)
        def _(t=t):
            left_copy(t).wait_send()


def apply_kernel(
    halves,
    per,
    dof,
    pay_ref,
    bins_ref,
    *refs,
):
    v_refs = refs[:halves]
    (out_ref, v_all, gat, power, edge, halo, sums, az_lo, az_hi) = refs[halves : halves + 9]
    (vsem, gsend, grecv, esend, erecv, asend, arecv) = refs[halves + 9 :]
    me = lax.axis_index("rng")
    az = lax.axis_index("az")
    n = lax.axis_size("rng")
    m = lax.axis_size("az")
    beams, num_chan, cells = out_ref.shape
    pulses, num_sel = v_all.shape[2], v_all.shape[3]
    taps = pulses * num_sel
    az_next = lax.rem(az + 1, m)
    az_prev = lax.rem(az + m - 1, m)
    barrier = pltpu.get_barrier_semaphore()
    for d in range(1, n):
        peer = lax.rem(me + d, n)
        pl.semaphore_signal(barrier, inc=1, device_id={"rng": peer}, device_id_type=MESH)
    for other in (az_next, az_prev):
        pl.semaphore_signal(barrier, inc=1, device_id={"az": other}, device_id_type=MESH)
    share = beams // halves
    loads = []
    for h in range(halves):
        load = pltpu.make_async_copy(v_refs[h], v_all.at[pl.ds(h * share, share)], vsem.at[h])
        load.start()
        loads.append(load)
    pl.semaphore_wait(barrier, n + 1)

    copies = []
    for d in range(1, n):
        peer = lax.rem(me + d, n)
        copy = pltpu.make_async_remote_copy(
            src_ref=pay_ref,
            dst_ref=gat.at[me],
            send_sem=gsend.at[d],
            recv_sem=grecv.at[d],
            device_id={"rng": peer},
            device_id_type=MESH,
        )
        copy.start()
        copies.append(copy)
    gat[me] = pay_ref[...]
    for load in loads:
        load.wait()
    for copy in copies:
        copy.wait_recv()
    rows = gat.shape[1] - beams
    count = jnp.zeros((beams, gat.shape[2]), jnp.float32)
    for r in range(n):
        count = count + gat[r, rows:, :]
    sums[0] = jnp.zeros(sums.shape[1:], jnp.float32)
    for b in range(beams):
        sums[b, :1, :] = count[b : b + 1]
    freq = lax.broadcasted_iota(jnp.int32, (num_chan, taps), 1) // num_sel
    lanes = gat.shape[2]
    lane = lax.broadcasted_iota(jnp.int32, (num_chan, lanes), 1)

    def one(b, carry):
        if per >= num_chan:
            ratio = per // num_chan
            start = pl.multiple_of((b % ratio) * num_chan, 8)
            w = gat[b // ratio, pl.ds(start, num_chan), :]
        else:
            split = num_chan // per
            w = jnp.concatenate([gat[b * split + t, :per, :] for t in range(split)], 0)
        w = w * sums[b, :1, :]
        quiet = w[:, 2 * dof : 2 * dof + 1]
        centre = bins_ref[b]
        planes = []
        hits = []
        for q in range(BINS):
            f = lax.rem(centre + (q - BINS // 2 + pulses), pulses)
            hits.append(freq == f)
        for part in range(2):
            plane = jnp.zeros((num_chan, taps), jnp.float32)
            for q in range(BINS):
                start = part * dof + q * num_sel
                piece = pltpu.roll(w, (lanes - start) % lanes, 1) if start else w
                piece = jnp.where(lane < num_sel, piece, 0.0)
                span = num_sel
                while span < lanes:
                    piece = piece + pltpu.roll(piece, span, 1)
                    span *= 2
                tiled = jnp.concatenate([piece] * (taps // lanes), 1)
                plane = jnp.where(hits[q], tiled, plane)
            planes.append(plane)
        top = jnp.concatenate([planes[0], planes[1]], 1)
        low = jnp.concatenate([-planes[1], planes[0]], 1)
        lhs = jnp.concatenate([top, low], 0).astype(jnp.bfloat16)
        flat = v_all[b].reshape(2 * taps, cells)
        proj = jnp.dot(lhs, flat, preferred_element_type=jnp.float32)
        p0 = proj[:num_chan]
        p1 = proj[num_chan:]
        power[b] = (p0 * p0 + p1 * p1) / quiet
        return carry

    lax.fori_loop(0, beams, one, 0)
    items = beams * num_chan
    turned = power[...].reshape(items, cells).T
    edge[0] = turned[:8]
    edge[1] = turned[cells - 8 :]

    def edge_copy(side):
        target = lax.rem(me + 1, n) if side else lax.rem(me + n - 1, n)
        return pltpu.make_async_remote_copy(
            src_ref=edge.at[side],
            dst_ref=halo.at[side],
            send_sem=esend.at[side],
            recv_sem=erecv.at[side],
            device_id={"rng": target},
            device_id_type=MESH,
        )

    for side in range(2):
        edge_copy(side).start()
    for side in range(2):
        edge_copy(side).wait()
    before = jnp.where(me > 0, halo[1, 7:8], 0.0)
    after = jnp.where(me < n - 1, halo[0, 0:1], 0.0)
    turned = (
        jnp.concatenate([before, turned[:-1]], 0)
        + turned
        + jnp.concatenate([turned[1:], after], 0)
    )
    sums[...] = turned.T.reshape(beams, num_chan, cells)
    up = pltpu.make_async_remote_copy(
        src_ref=sums.at[beams - 1],
        dst_ref=az_lo,
        send_sem=asend.at[0],
        recv_sem=arecv.at[0],
        device_id={"az": az_next},
        device_id_type=MESH,
    )
    down = pltpu.make_async_remote_copy(
        src_ref=sums.at[0],
        dst_ref=az_hi,
        send_sem=asend.at[1],
        recv_sem=arecv.at[1],
        device_id={"az": az_prev},
        device_id_type=MESH,
    )
    up.start()
    down.start()
    for b in range(1, beams - 1):
        out_ref[b] = (sums[b - 1] + sums[b] + sums[b + 1]) / 9.0
    up.wait_recv()
    down.wait_recv()
    out_ref[0] = (az_lo[...] + sums[0] + sums[1]) / 9.0
    out_ref[beams - 1] = (sums[beams - 2] + sums[beams - 1] + az_hi[...]) / 9.0
    up.wait_send()
    down.wait_send()
    for copy in copies:
        copy.wait_send()


def body(echoes, arc_start, arc_offsets, doppler_bins, steer_angles, train_mask):
    columns = echoes.shape[1]
    num_pulses = echoes.shape[2]
    cells = echoes.shape[3]
    num_sel = arc_offsets.shape[1]
    chan_count = doppler_bins.shape[1]
    cycle_size = lax.axis_size("az")
    cycle_pos = lax.axis_index("az")
    rng_size = lax.axis_size("rng")
    beam_count = BEAMS // cycle_size
    item_count = beam_count * chan_count
    dof = BINS * num_sel
    table_re, table_im = doppler_table(num_pulses)
    table = jnp.concatenate(
        [jnp.concatenate([table_re, -table_im], 1), jnp.concatenate([table_im, table_re], 1)], 0
    )

    def own(x):
        return lax.dynamic_slice_in_dim(x, cycle_pos * beam_count, beam_count, axis=0)

    arc_first = (own(arc_start) - cycle_pos * columns + ARC // 2) % COLS
    col_index = arc_first[:, None] + own(arc_offsets)
    bins_own = own(doppler_bins)
    angles = own(steer_angles)
    block_count = train_mask.shape[1]
    cell_mask = (
        jnp.broadcast_to(train_mask[:, :, None], (beam_count, block_count, BLK))
        .reshape(beam_count, 1, block_count * BLK)
        .astype(jnp.bfloat16)
    )
    smem = pl.BlockSpec(memory_space=pltpu.SMEM)

    def snap_gram(extended, first, last, base):
        share = last - first
        ext_cols = extended.shape[1]
        return pl.pallas_call(
            snap_gram_kernel,
            grid=(share,),
            in_specs=[
                smem,
                smem,
                smem,
                smem,
                pl.BlockSpec((2, ext_cols, num_pulses, cells), lambda b: (0, 0, 0, 0)),
                pl.BlockSpec(table.shape, lambda b: (0, 0)),
                pl.BlockSpec((1, 1, cells), lambda b: (b, 0, 0)),
            ],
            out_specs=[
                pl.BlockSpec((1, 2, num_pulses, num_sel, cells), lambda b: (b, 0, 0, 0, 0)),
                pl.BlockSpec((1, dof, chan_count * dof), lambda b: (b, 0, 0)),
            ],
            out_shape=[
                jax.ShapeDtypeStruct((share, 2, num_pulses, num_sel, cells), jnp.bfloat16),
                jax.ShapeDtypeStruct((share, dof, chan_count * dof), jnp.float32),
            ],
            compiler_params=pltpu.CompilerParams(vmem_limit_bytes=VMEM_LIMIT),
            cost_estimate=pl.CostEstimate(
                flops=share * 600_000_000, bytes_accessed=share * 1_500_000, transcendentals=0
            ),
            name="snap_gram",
        )(
            col_index[first:last] - base,
            bins_own[first:last],
            jnp.cos(angles)[first:last],
            jnp.sin(angles)[first:last],
            extended,
            table,
            cell_mask[first:last],
        )

    width = ARC // 2
    forward = [(i, (i + 1) % cycle_size) for i in range(cycle_size)]
    backward = [(target, source) for source, target in forward]
    low = lax.ppermute(echoes[:, columns - width :], "az", forward)
    high = lax.ppermute(echoes[:, :width], "az", backward)
    step = COLS // BEAMS
    half = beam_count // 2
    if (half - 1) * step + step - 1 + ARC - 1 < width + columns and half * step >= width:
        v_lo, gram_lo = snap_gram(jnp.concatenate([low, echoes], 1), 0, half, 0)
        high, v_lo, gram_lo = lax.optimization_barrier((high, v_lo, gram_lo))
        v_hi, gram_hi = snap_gram(jnp.concatenate([echoes, high], 1), half, beam_count, width)
        v_parts = (v_lo, v_hi)
        gram = jnp.concatenate([gram_lo, gram_hi], 0)
    else:
        v_one, gram = snap_gram(jnp.concatenate([low, echoes, high], 1), 0, beam_count, 0)
        v_parts = (v_one,)

    per = item_count // rng_size
    if per < chan_count:
        split = chan_count // per
        gram = gram.reshape(beam_count, dof, split, per * dof)
        gram = jnp.swapaxes(gram, 1, 2).reshape(beam_count * split, dof, per * dof)
        width = per
    else:
        width = chan_count
    vm = pltpu.VMEM
    dma = pltpu.SemaphoreType.DMA
    line = rng_size // 2
    chunk = (gram.shape[0] // rng_size, dof, gram.shape[2])
    part = pl.pallas_call(
        functools.partial(scatter_kernel, line),
        in_specs=[pl.BlockSpec(memory_space=vm)],
        out_specs=pl.BlockSpec(memory_space=vm),
        out_shape=jax.ShapeDtypeStruct(chunk, jnp.float32),
        scratch_shapes=[vm((line,) + chunk, jnp.float32)] * 4 + [dma((line,))] * 6,
        compiler_params=pltpu.CompilerParams(
            collective_id=0, has_side_effects=True, vmem_limit_bytes=VMEM_LIMIT
        ),
        name="scatter",
    )(gram.reshape((rng_size,) + chunk))
    lead = part.shape[0]
    mats = part.reshape(lead, dof, width, dof).transpose(1, 3, 0, 2).reshape(dof, dof, per)
    flip = jnp.swapaxes(mats, 0, 1)
    ids = jnp.arange(dof, dtype=jnp.int32)
    row, col = ids[:, None, None], ids[None, :, None]
    h_re = jnp.where(row >= col, mats, flip)
    h_im = jnp.where(row < col, mats, jnp.where(row > col, -flip, 0.0))
    solved = pl.pallas_call(
        solve_kernel,
        out_shape=jax.ShapeDtypeStruct((2 * dof + 8, per), jnp.float32),
        scratch_shapes=[
            vm((dof, dof + 8, per), jnp.float32),
            vm((dof, dof + 8, per), jnp.float32),
            vm((dof, per), jnp.float32),
            vm((dof, per), jnp.float32),
        ],
        compiler_params=pltpu.CompilerParams(vmem_limit_bytes=VMEM_LIMIT),
        name="solve",
    )(h_re, h_im)
    lanes = 128
    local_count = (BLK * jnp.sum(train_mask, axis=1)).astype(jnp.float32)
    pad_rows = -per % 8
    payload = jnp.concatenate(
        [
            jnp.pad(solved.T, ((0, pad_rows), (0, lanes - solved.shape[0]))),
            jnp.broadcast_to(local_count[:, None], (beam_count, lanes)),
        ],
        0,
    )
    halves = len(v_parts)
    any_spec = pl.BlockSpec(memory_space=pl.ANY)
    block = (chan_count, cells)
    out = pl.pallas_call(
        functools.partial(apply_kernel, halves, per, dof),
        in_specs=[pl.BlockSpec(memory_space=vm)] * 2 + [any_spec] * halves,
        out_specs=pl.BlockSpec(memory_space=vm),
        out_shape=jax.ShapeDtypeStruct((beam_count,) + block, jnp.float32),
        scratch_shapes=[
            vm((beam_count, 2, num_pulses, num_sel, cells), jnp.bfloat16),
            vm((rng_size,) + payload.shape, jnp.float32),
            vm((beam_count,) + block, jnp.float32),
            vm((2, 8, item_count), jnp.float32),
            vm((2, 8, item_count), jnp.float32),
            vm((beam_count,) + block, jnp.float32),
            vm(block, jnp.float32),
            vm(block, jnp.float32),
            dma((halves,)),
            dma((rng_size,)),
            dma((rng_size,)),
            dma((2,)),
            dma((2,)),
            dma((2,)),
            dma((2,)),
        ],
        compiler_params=pltpu.CompilerParams(
            collective_id=1, has_side_effects=True, vmem_limit_bytes=VMEM_LIMIT
        ),
        name="apply",
    )(payload, bins_own[:, :, None], *v_parts)
    return out


def solution(mesh):
    return jax.shard_map(
        body,
        mesh=mesh,
        in_specs=(P(None, "az", None, "rng"), P(), P(), P(), P(), P("az", "rng")),
        out_specs=P("az", None, "rng"),
        check_vma=False,
    )
```

```python
import functools

import jax
import jax.numpy as jnp
from jax import lax
from jax.experimental import pallas as pl
from jax.experimental.pallas import tpu as pltpu
from jax.sharding import PartitionSpec as P


COLS = 256
ARC = 64
BINS = 3
BEAMS = 64
BLK = 128
LOADING = 0.1
VMEM_LIMIT = 48 << 20


def doppler_table(num_pulses):
    freq_ids = jnp.arange(num_pulses, dtype=jnp.int32)
    phase_steps = freq_ids[:, None] * freq_ids[None, :] % num_pulses
    phase_angle = -2.0 * jnp.pi / num_pulses * phase_steps.astype(jnp.float32)
    return (jnp.cos(phase_angle).astype(jnp.bfloat16), jnp.sin(phase_angle).astype(jnp.bfloat16))


def snap_gram_kernel(
    col_ref, bins_ref, cos_ref, sin_ref, ext_ref, table_ref, mask_ref, v_ref, gram_ref
):
    beam = pl.program_id(0)
    pulses = ext_ref.shape[2]
    num_sel = col_ref.shape[1]
    num_chan = bins_ref.shape[1]
    table = table_ref[...]
    parts_re, parts_im = [], []
    for j in range(num_sel):
        col = col_ref[beam, j]
        data = jnp.concatenate([ext_ref[0, col], ext_ref[1, col]], axis=0)
        spec = jnp.dot(table, data, preferred_element_type=jnp.float32)
        cosine = cos_ref[beam, j]
        sine = sin_ref[beam, j]
        spec_re = spec[:pulses]
        spec_im = spec[pulses:]
        parts_re.append(cosine * spec_re - sine * spec_im)
        parts_im.append(sine * spec_re + cosine * spec_im)
    for part, pieces in enumerate((parts_re, parts_im)):
        stacked = jnp.swapaxes(jnp.stack(pieces, 0), 0, 1)
        v_ref[0, part] = stacked.astype(jnp.bfloat16)
    dof = BINS * num_sel
    mask_row = mask_ref[0]
    row = lax.broadcasted_iota(jnp.int32, (dof, dof), 0)
    colm = lax.broadcasted_iota(jnp.int32, (dof, dof), 1)
    lower = row >= colm
    packed = []
    for k in range(num_chan):
        centre = bins_ref[beam, k]
        ids = [(centre + (q - BINS // 2 + pulses)) % pulses for q in range(BINS)]
        u_re = jnp.concatenate([v_ref[0, 0, f] for f in ids], 0)
        u_im = jnp.concatenate([v_ref[0, 1, f] for f in ids], 0)
        right = jnp.concatenate([u_re, u_im], 1)
        m_re = u_re * mask_row
        m_im = u_im * mask_row
        left = jnp.concatenate(
            [jnp.concatenate([m_re, m_im], 1), jnp.concatenate([m_im, -m_re], 1)], 0
        )
        both = lax.dot_general(
            left, right, (((1,), (1,)), ((), ())), preferred_element_type=jnp.float32
        )
        packed.append(jnp.where(lower, both[:dof], both[dof:]))
    gram_ref[0] = jnp.concatenate(packed, 1)


def solve_kernel(part_ref, out_ref, stack, turned, h, x1, x2):
    lead, dof, wide = part_ref.shape
    width = wide // dof
    lanes = lead * width
    nb = dof // 8
    group = min(8, lanes)
    for g in range(0, lanes, group):
        pieces = []
        for item in range(g, g + group):
            k = item % width
            pieces.append(part_ref[item // width, :, k * dof : (k + 1) * dof])
        stack[:, g : g + group, :] = jnp.swapaxes(jnp.stack(pieces, 0), 0, 1)
    for i in range(dof):
        turned[i] = stack[i].T
    trace = jnp.zeros((1, lanes), jnp.float32)
    for i in range(dof):
        trace = trace + turned[i, i : i + 1, :]
    load = (LOADING / dof) * trace
    cube = (8, 8, lanes)
    row = lax.broadcasted_iota(jnp.int32, cube, 0)
    col = lax.broadcasted_iota(jnp.int32, cube, 1)
    for ib in range(nb):
        rows = slice(8 * ib, 8 * ib + 8)
        for jb in range(ib, nb):
            cols = slice(8 * jb, 8 * jb + 8)
            imag = turned[rows, cols, :]
            real = jnp.swapaxes(turned[cols, rows, :], 0, 1)
            if ib == jb:
                straight, flip = imag, real
                real = jnp.where(row >= col, straight, flip)
                real = jnp.where(row == col, real + load[None], real)
                imag = jnp.where(row < col, straight, jnp.where(row > col, -flip, 0.0))
            h[rows, cols, :] = jnp.concatenate([real, imag], 2)
    h[:, dof:, :] = jnp.concatenate(
        [jnp.ones((dof, 8, lanes), jnp.float32), jnp.zeros((dof, 8, lanes), jnp.float32)], 2
    )
    x1[...] = jnp.zeros_like(x1)
    x2[...] = jnp.zeros_like(x2)
    sub = lax.broadcasted_iota(jnp.int32, (8, 2 * lanes), 0)

    for kb in range(nb):

        def step(k, carry, kb=kb):
            pivot = 1.0 / h[k, pl.ds(k, 1), :][:, :lanes]
            pivot = jnp.concatenate([pivot, pivot], 1)
            straight = [h[k, 8 * b : 8 * b + 8, :] for b in range(kb, nb + 1)]
            real = [p[:, :lanes] for p in straight]
            imag = [p[:, lanes:] for p in straight]
            turn = [jnp.concatenate([-i, r], 1) for r, i in zip(real, imag)]
            for ib in range(kb, nb):
                r, i = real[ib - kb], imag[ib - kb]
                fr = jnp.concatenate([r, r], 1) * pivot
                fi = jnp.concatenate([i, i], 1) * -pivot
                if ib == kb:
                    live = sub + 8 * kb > k
                    fr = jnp.where(live, fr, 0.0)
                    fi = jnp.where(live, fi, 0.0)
                for s in range(8):
                    t = 8 * ib + s
                    cr = jnp.broadcast_to(fr[s : s + 1], (8, 2 * lanes))
                    ci = jnp.broadcast_to(fi[s : s + 1], (8, 2 * lanes))
                    for b in range(ib, nb + 1):
                        sl = slice(8 * b, 8 * b + 8)
                        h[t, sl, :] = h[t, sl, :] - (cr * straight[b - kb] + ci * turn[b - kb])
            return carry

        lax.fori_loop(8 * kb, 8 * kb + 8, step, 0)

    for ib in reversed(range(nb)):

        def back(t, carry, ib=ib):
            i = 8 * ib + 7 - t
            u = jnp.zeros((8, 2 * lanes), jnp.float32)
            v = jnp.zeros((8, 2 * lanes), jnp.float32)
            for b in range(ib, nb):
                sl = slice(8 * b, 8 * b + 8)
                line = h[i, sl, :]
                u = u + line * x1[sl, :]
                v = v + line * x2[sl, :]
            u = jnp.sum(u, 0, keepdims=True)
            v = jnp.sum(v, 0, keepdims=True)
            pivot = 1.0 / h[i, pl.ds(i, 1), :][:, :lanes]
            top = h[i, dof : dof + 1, :]
            re = (top[:, :lanes] - (u[:, :lanes] + u[:, lanes:])) * pivot
            im = (top[:, lanes:] - (v[:, :lanes] + v[:, lanes:])) * pivot
            x1[pl.ds(i, 1), :] = jnp.concatenate([re, -im], 1)
            x2[pl.ds(i, 1), :] = jnp.concatenate([im, re], 1)
            return carry

        lax.fori_loop(0, 8, back, 0)
    re = x1[:, :lanes]
    out_ref[:dof, :] = re
    out_ref[dof : 2 * dof, :] = x2[:, :lanes]
    out_ref[2 * dof :, :] = jnp.broadcast_to(jnp.sum(re, 0, keepdims=True), (8, lanes))


MESH = pl.DeviceIdType.MESH


def scatter_kernel(n, g_ref, out_ref, pair, acc, right, left, psend, precv, rsend, rrecv, lsend, lrecv):
    me = lax.axis_index("rng")
    z = me // 2
    c = me % 2
    mate = 2 * z + 1 - c
    ahead = lax.rem(me + 2, 2 * n)
    behind = lax.rem(me + 2 * n - 2, 2 * n)
    barrier = pltpu.get_barrier_semaphore()
    pl.semaphore_signal(barrier, inc=1, device_id={"rng": mate}, device_id_type=MESH)
    pl.semaphore_signal(barrier, inc=1, device_id={"rng": ahead}, device_id_type=MESH)
    pl.semaphore_signal(barrier, inc=1, device_id={"rng": behind}, device_id_type=MESH)
    pl.semaphore_wait(barrier, 3)

    order = []
    for t in range((n + 1) // 2):
        order.append(n - 1 - t)
        if t != n - 1 - t:
            order.append(t)

    def pair_copy(t):
        return pltpu.make_async_remote_copy(
            src_ref=g_ref.at[2 * t + 1 - c],
            dst_ref=pair.at[t],
            send_sem=psend.at[t],
            recv_sem=precv.at[t],
            device_id={"rng": mate},
            device_id_type=MESH,
        )

    def right_copy(t):
        return pltpu.make_async_remote_copy(
            src_ref=acc.at[t],
            dst_ref=right.at[t],
            send_sem=rsend.at[t],
            recv_sem=rrecv.at[t],
            device_id={"rng": ahead},
            device_id_type=MESH,
        )

    def left_copy(t):
        return pltpu.make_async_remote_copy(
            src_ref=acc.at[t],
            dst_ref=left.at[t],
            send_sem=lsend.at[t],
            recv_sem=lrecv.at[t],
            device_id={"rng": behind},
            device_id_type=MESH,
        )

    for t in order:
        pair_copy(t).start()
    for t in order:
        pair_copy(t).wait_recv()
        acc[t] = g_ref[2 * t + c] + pair[t]

        @pl.when(jnp.logical_and(z == 0, t > 0))
        def _(t=t):
            right_copy(t).start()

        @pl.when(jnp.logical_and(z == n - 1, t < n - 1))
        def _(t=t):
            left_copy(t).start()

    for place in range(n):
        events = [(place + n - 1 - t, 0, t) for t in range(place + 1, n) if place > 0]
        events += [(n - 1 - place + t, 1, t) for t in range(place) if place < n - 1]

        @pl.when(z == place)
        def _(place=place, events=sorted(events)):
            for _, side, t in events:
                copy = left_copy(t) if side else right_copy(t)
                source = left if side else right
                copy.wait_recv()
                acc[t] = acc[t] + source[t]
                copy.start()
            total = acc[place]
            if place > 0:
                right_copy(place).wait_recv()
                total = total + right[place]
            if place < n - 1:
                left_copy(place).wait_recv()
                total = total + left[place]
            out_ref[...] = total

    for t in range(n):
        pair_copy(t).wait_send()

        @pl.when(z < t)
        def _(t=t):
            right_copy(t).wait_send()

        @pl.when(z > t)
        def _(t=t):
            left_copy(t).wait_send()


def apply_kernel(
    halves,
    per,
    dof,
    pay_ref,
    bins_ref,
    *refs,
):
    v_refs = refs[:halves]
    (out_ref, v_all, gat, power, edge, halo, sums, az_lo, az_hi) = refs[halves : halves + 9]
    (vsem, gsend, grecv, esend, erecv, asend, arecv) = refs[halves + 9 :]
    me = lax.axis_index("rng")
    az = lax.axis_index("az")
    n = lax.axis_size("rng")
    m = lax.axis_size("az")
    beams, num_chan, cells = out_ref.shape
    pulses, num_sel = v_all.shape[2], v_all.shape[3]
    taps = pulses * num_sel
    az_next = lax.rem(az + 1, m)
    az_prev = lax.rem(az + m - 1, m)
    barrier = pltpu.get_barrier_semaphore()
    for d in range(1, n):
        peer = lax.rem(me + d, n)
        pl.semaphore_signal(barrier, inc=1, device_id={"rng": peer}, device_id_type=MESH)
    for other in (az_next, az_prev):
        pl.semaphore_signal(barrier, inc=1, device_id={"az": other}, device_id_type=MESH)
    share = beams // halves
    loads = []
    for h in range(halves):
        load = pltpu.make_async_copy(v_refs[h], v_all.at[pl.ds(h * share, share)], vsem.at[h])
        load.start()
        loads.append(load)
    pl.semaphore_wait(barrier, n + 1)

    copies = []
    for d in range(1, n):
        peer = lax.rem(me + d, n)
        copy = pltpu.make_async_remote_copy(
            src_ref=pay_ref,
            dst_ref=gat.at[me],
            send_sem=gsend.at[d],
            recv_sem=grecv.at[d],
            device_id={"rng": peer},
            device_id_type=MESH,
        )
        copy.start()
        copies.append(copy)
    gat[me] = pay_ref[...]
    for load in loads:
        load.wait()
    for copy in copies:
        copy.wait_recv()
    rows = gat.shape[1] - beams
    count = jnp.zeros((beams, gat.shape[2]), jnp.float32)
    for r in range(n):
        count = count + gat[r, rows:, :]
    sums[0] = jnp.zeros(sums.shape[1:], jnp.float32)
    for b in range(beams):
        sums[b, :1, :] = count[b : b + 1]
    freq = lax.broadcasted_iota(jnp.int32, (num_chan, taps), 1) // num_sel
    lanes = gat.shape[2]
    lane = lax.broadcasted_iota(jnp.int32, (num_chan, lanes), 1)

    def one(b, carry):
        if per >= num_chan:
            ratio = per // num_chan
            start = pl.multiple_of((b % ratio) * num_chan, 8)
            w = gat[b // ratio, pl.ds(start, num_chan), :]
        else:
            split = num_chan // per
            w = jnp.concatenate([gat[b * split + t, :per, :] for t in range(split)], 0)
        w = w * sums[b, :1, :]
        quiet = w[:, 2 * dof : 2 * dof + 1]
        centre = bins_ref[b]
        planes = []
        hits = []
        for q in range(BINS):
            f = lax.rem(centre + (q - BINS // 2 + pulses), pulses)
            hits.append(freq == f)
        for part in range(2):
            plane = jnp.zeros((num_chan, taps), jnp.float32)
            for q in range(BINS):
                start = part * dof + q * num_sel
                piece = pltpu.roll(w, (lanes - start) % lanes, 1) if start else w
                piece = jnp.where(lane < num_sel, piece, 0.0)
                span = num_sel
                while span < lanes:
                    piece = piece + pltpu.roll(piece, span, 1)
                    span *= 2
                tiled = jnp.concatenate([piece] * (taps // lanes), 1)
                plane = jnp.where(hits[q], tiled, plane)
            planes.append(plane)
        top = jnp.concatenate([planes[0], planes[1]], 1)
        low = jnp.concatenate([-planes[1], planes[0]], 1)
        lhs = jnp.concatenate([top, low], 0).astype(jnp.bfloat16)
        flat = v_all[b].reshape(2 * taps, cells)
        proj = jnp.dot(lhs, flat, preferred_element_type=jnp.float32)
        p0 = proj[:num_chan]
        p1 = proj[num_chan:]
        power[b] = (p0 * p0 + p1 * p1) / quiet
        return carry

    lax.fori_loop(0, beams, one, 0)
    items = beams * num_chan
    turned = power[...].reshape(items, cells).T
    edge[0] = turned[:8]
    edge[1] = turned[cells - 8 :]

    def edge_copy(side):
        target = lax.rem(me + 1, n) if side else lax.rem(me + n - 1, n)
        return pltpu.make_async_remote_copy(
            src_ref=edge.at[side],
            dst_ref=halo.at[side],
            send_sem=esend.at[side],
            recv_sem=erecv.at[side],
            device_id={"rng": target},
            device_id_type=MESH,
        )

    for side in range(2):
        edge_copy(side).start()
    for side in range(2):
        edge_copy(side).wait()
    before = jnp.where(me > 0, halo[1, 7:8], 0.0)
    after = jnp.where(me < n - 1, halo[0, 0:1], 0.0)
    turned = (
        jnp.concatenate([before, turned[:-1]], 0)
        + turned
        + jnp.concatenate([turned[1:], after], 0)
    )
    sums[...] = turned.T.reshape(beams, num_chan, cells)
    up = pltpu.make_async_remote_copy(
        src_ref=sums.at[beams - 1],
        dst_ref=az_lo,
        send_sem=asend.at[0],
        recv_sem=arecv.at[0],
        device_id={"az": az_next},
        device_id_type=MESH,
    )
    down = pltpu.make_async_remote_copy(
        src_ref=sums.at[0],
        dst_ref=az_hi,
        send_sem=asend.at[1],
        recv_sem=arecv.at[1],
        device_id={"az": az_prev},
        device_id_type=MESH,
    )
    up.start()
    down.start()
    for b in range(1, beams - 1):
        out_ref[b] = (sums[b - 1] + sums[b] + sums[b + 1]) / 9.0
    up.wait_recv()
    down.wait_recv()
    out_ref[0] = (az_lo[...] + sums[0] + sums[1]) / 9.0
    out_ref[beams - 1] = (sums[beams - 2] + sums[beams - 1] + az_hi[...]) / 9.0
    up.wait_send()
    down.wait_send()
    for copy in copies:
        copy.wait_send()


def body(echoes, arc_start, arc_offsets, doppler_bins, steer_angles, train_mask):
    columns = echoes.shape[1]
    num_pulses = echoes.shape[2]
    cells = echoes.shape[3]
    num_sel = arc_offsets.shape[1]
    chan_count = doppler_bins.shape[1]
    cycle_size = lax.axis_size("az")
    cycle_pos = lax.axis_index("az")
    rng_size = lax.axis_size("rng")
    beam_count = BEAMS // cycle_size
    item_count = beam_count * chan_count
    dof = BINS * num_sel
    table_re, table_im = doppler_table(num_pulses)
    table = jnp.concatenate(
        [jnp.concatenate([table_re, -table_im], 1), jnp.concatenate([table_im, table_re], 1)], 0
    )

    def own(x):
        return lax.dynamic_slice_in_dim(x, cycle_pos * beam_count, beam_count, axis=0)

    arc_first = (own(arc_start) - cycle_pos * columns + ARC // 2) % COLS
    col_index = arc_first[:, None] + own(arc_offsets)
    bins_own = own(doppler_bins)
    angles = own(steer_angles)
    block_count = train_mask.shape[1]
    cell_mask = (
        jnp.broadcast_to(train_mask[:, :, None], (beam_count, block_count, BLK))
        .reshape(beam_count, 1, block_count * BLK)
        .astype(jnp.bfloat16)
    )
    smem = pl.BlockSpec(memory_space=pltpu.SMEM)

    def snap_gram(extended, first, last, base):
        share = last - first
        ext_cols = extended.shape[1]
        return pl.pallas_call(
            snap_gram_kernel,
            grid=(share,),
            in_specs=[
                smem,
                smem,
                smem,
                smem,
                pl.BlockSpec((2, ext_cols, num_pulses, cells), lambda b: (0, 0, 0, 0)),
                pl.BlockSpec(table.shape, lambda b: (0, 0)),
                pl.BlockSpec((1, 1, cells), lambda b: (b, 0, 0)),
            ],
            out_specs=[
                pl.BlockSpec((1, 2, num_pulses, num_sel, cells), lambda b: (b, 0, 0, 0, 0)),
                pl.BlockSpec((1, dof, chan_count * dof), lambda b: (b, 0, 0)),
            ],
            out_shape=[
                jax.ShapeDtypeStruct((share, 2, num_pulses, num_sel, cells), jnp.bfloat16),
                jax.ShapeDtypeStruct((share, dof, chan_count * dof), jnp.float32),
            ],
            compiler_params=pltpu.CompilerParams(vmem_limit_bytes=VMEM_LIMIT),
            cost_estimate=pl.CostEstimate(
                flops=share * 600_000_000, bytes_accessed=share * 1_500_000, transcendentals=0
            ),
            name="snap_gram",
        )(
            col_index[first:last] - base,
            bins_own[first:last],
            jnp.cos(angles)[first:last],
            jnp.sin(angles)[first:last],
            extended,
            table,
            cell_mask[first:last],
        )

    width = ARC // 2
    forward = [(i, (i + 1) % cycle_size) for i in range(cycle_size)]
    backward = [(target, source) for source, target in forward]
    low = lax.ppermute(echoes[:, columns - width :], "az", forward)
    high = lax.ppermute(echoes[:, :width], "az", backward)
    step = COLS // BEAMS
    half = beam_count // 2
    if (half - 1) * step + step - 1 + ARC - 1 < width + columns and half * step >= width:
        v_lo, gram_lo = snap_gram(jnp.concatenate([low, echoes], 1), 0, half, 0)
        high, v_lo, gram_lo = lax.optimization_barrier((high, v_lo, gram_lo))
        v_hi, gram_hi = snap_gram(jnp.concatenate([echoes, high], 1), half, beam_count, width)
        v_parts = (v_lo, v_hi)
        gram = jnp.concatenate([gram_lo, gram_hi], 0)
    else:
        v_one, gram = snap_gram(jnp.concatenate([low, echoes, high], 1), 0, beam_count, 0)
        v_parts = (v_one,)

    per = item_count // rng_size
    if per < chan_count:
        split = chan_count // per
        gram = gram.reshape(beam_count, dof, split, per * dof)
        gram = jnp.swapaxes(gram, 1, 2).reshape(beam_count * split, dof, per * dof)
        width = per
    else:
        width = chan_count
    vm = pltpu.VMEM
    dma = pltpu.SemaphoreType.DMA
    line = rng_size // 2
    chunk = (gram.shape[0] // rng_size, dof, gram.shape[2])
    part = pl.pallas_call(
        functools.partial(scatter_kernel, line),
        in_specs=[pl.BlockSpec(memory_space=vm)],
        out_specs=pl.BlockSpec(memory_space=vm),
        out_shape=jax.ShapeDtypeStruct(chunk, jnp.float32),
        scratch_shapes=[vm((line,) + chunk, jnp.float32)] * 4 + [dma((line,))] * 6,
        compiler_params=pltpu.CompilerParams(
            collective_id=0, has_side_effects=True, vmem_limit_bytes=VMEM_LIMIT
        ),
        name="scatter",
    )(gram.reshape((rng_size,) + chunk))
    solved = pl.pallas_call(
        solve_kernel,
        out_shape=jax.ShapeDtypeStruct((2 * dof + 8, per), jnp.float32),
        scratch_shapes=[
            vm((dof, per, dof), jnp.float32),
            vm((dof, dof, per), jnp.float32),
            vm((dof, dof + 8, 2 * per), jnp.float32),
            vm((dof, 2 * per), jnp.float32),
            vm((dof, 2 * per), jnp.float32),
        ],
        compiler_params=pltpu.CompilerParams(vmem_limit_bytes=VMEM_LIMIT),
        name="solve",
    )(part)
    lanes = 128
    local_count = (BLK * jnp.sum(train_mask, axis=1)).astype(jnp.float32)
    pad_rows = -per % 8
    payload = jnp.concatenate(
        [
            jnp.pad(solved.T, ((0, pad_rows), (0, lanes - solved.shape[0]))),
            jnp.broadcast_to(local_count[:, None], (beam_count, lanes)),
        ],
        0,
    )
    halves = len(v_parts)
    any_spec = pl.BlockSpec(memory_space=pl.ANY)
    block = (chan_count, cells)
    out = pl.pallas_call(
        functools.partial(apply_kernel, halves, per, dof),
        in_specs=[pl.BlockSpec(memory_space=vm)] * 2 + [any_spec] * halves,
        out_specs=pl.BlockSpec(memory_space=vm),
        out_shape=jax.ShapeDtypeStruct((beam_count,) + block, jnp.float32),
        scratch_shapes=[
            vm((beam_count, 2, num_pulses, num_sel, cells), jnp.bfloat16),
            vm((rng_size,) + payload.shape, jnp.float32),
            vm((beam_count,) + block, jnp.float32),
            vm((2, 8, item_count), jnp.float32),
            vm((2, 8, item_count), jnp.float32),
            vm((beam_count,) + block, jnp.float32),
            vm(block, jnp.float32),
            vm(block, jnp.float32),
            dma((halves,)),
            dma((rng_size,)),
            dma((rng_size,)),
            dma((2,)),
            dma((2,)),
            dma((2,)),
            dma((2,)),
        ],
        compiler_params=pltpu.CompilerParams(
            collective_id=1, has_side_effects=True, vmem_limit_bytes=VMEM_LIMIT
        ),
        name="apply",
    )(payload, bins_own[:, :, None], *v_parts)
    return out


def solution(mesh):
    return jax.shard_map(
        body,
        mesh=mesh,
        in_specs=(P(None, "az", None, "rng"), P(), P(), P(), P(), P("az", "rng")),
        out_specs=P("az", None, "rng"),
        check_vma=False,
    )
```

```python
import functools

import jax
import jax.numpy as jnp
from jax import lax
from jax.experimental import pallas as pl
from jax.experimental.pallas import tpu as pltpu
from jax.sharding import PartitionSpec as P


COLS = 256
ARC = 64
BINS = 3
BEAMS = 64
BLK = 128
LOADING = 0.1
VMEM_LIMIT = 48 << 20


def doppler_table(num_pulses):
    freq_ids = jnp.arange(num_pulses, dtype=jnp.int32)
    phase_steps = freq_ids[:, None] * freq_ids[None, :] % num_pulses
    phase_angle = -2.0 * jnp.pi / num_pulses * phase_steps.astype(jnp.float32)
    return (jnp.cos(phase_angle).astype(jnp.bfloat16), jnp.sin(phase_angle).astype(jnp.bfloat16))


def snap_gram_kernel(
    col_ref, bins_ref, cos_ref, sin_ref, ext_ref, table_ref, mask_ref, v_ref, gram_ref
):
    beam = pl.program_id(0)
    pulses = ext_ref.shape[2]
    num_sel = col_ref.shape[1]
    num_chan = bins_ref.shape[1]
    table = table_ref[...]
    parts_re, parts_im = [], []
    for j in range(num_sel):
        col = col_ref[beam, j]
        data = jnp.concatenate([ext_ref[0, col], ext_ref[1, col]], axis=0)
        spec = jnp.dot(table, data, preferred_element_type=jnp.float32)
        cosine = cos_ref[beam, j]
        sine = sin_ref[beam, j]
        spec_re = spec[:pulses]
        spec_im = spec[pulses:]
        parts_re.append(cosine * spec_re - sine * spec_im)
        parts_im.append(sine * spec_re + cosine * spec_im)
    for part, pieces in enumerate((parts_re, parts_im)):
        stacked = jnp.swapaxes(jnp.stack(pieces, 0), 0, 1)
        v_ref[0, part] = stacked.astype(jnp.bfloat16)
    dof = BINS * num_sel
    mask_row = mask_ref[0]
    row = lax.broadcasted_iota(jnp.int32, (dof, dof), 0)
    colm = lax.broadcasted_iota(jnp.int32, (dof, dof), 1)
    lower = row >= colm
    packed = []
    for k in range(num_chan):
        centre = bins_ref[beam, k]
        ids = [(centre + (q - BINS // 2 + pulses)) % pulses for q in range(BINS)]
        u_re = jnp.concatenate([v_ref[0, 0, f] for f in ids], 0)
        u_im = jnp.concatenate([v_ref[0, 1, f] for f in ids], 0)
        right = jnp.concatenate([u_re, u_im], 1)
        m_re = u_re * mask_row
        m_im = u_im * mask_row
        left = jnp.concatenate(
            [jnp.concatenate([m_re, m_im], 1), jnp.concatenate([m_im, -m_re], 1)], 0
        )
        both = lax.dot_general(
            left, right, (((1,), (1,)), ((), ())), preferred_element_type=jnp.float32
        )
        packed.append(jnp.where(lower, both[:dof], both[dof:]))
    gram_ref[0] = jnp.concatenate(packed, 1)


def solve_kernel(part_ref, out_ref, stack, turned, hr, hi, xr, xi):
    lead, dof, wide = part_ref.shape
    width = wide // dof
    lanes = lead * width
    nb = dof // 8
    group = min(8, lanes)
    for g in range(0, lanes, group):
        pieces = []
        for item in range(g, g + group):
            k = item % width
            pieces.append(part_ref[item // width, :, k * dof : (k + 1) * dof])
        stack[:, g : g + group, :] = jnp.swapaxes(jnp.stack(pieces, 0), 0, 1)
    for i in range(dof):
        turned[i] = stack[i].T
    trace = jnp.zeros((1, lanes), jnp.float32)
    for i in range(dof):
        trace = trace + turned[i, i : i + 1, :]
    load = (LOADING / dof) * trace
    cube = (8, 8, lanes)
    row = lax.broadcasted_iota(jnp.int32, cube, 0)
    col = lax.broadcasted_iota(jnp.int32, cube, 1)
    for ib in range(nb):
        rows = slice(8 * ib, 8 * ib + 8)
        for jb in range(ib, nb):
            cols = slice(8 * jb, 8 * jb + 8)
            imag = turned[rows, cols, :]
            real = jnp.swapaxes(turned[cols, rows, :], 0, 1)
            if ib == jb:
                straight, flip = imag, real
                real = jnp.where(row >= col, straight, flip)
                real = jnp.where(row == col, real + load[None], real)
                imag = jnp.where(row < col, straight, jnp.where(row > col, -flip, 0.0))
            hr[rows, cols, :] = real
            hi[rows, cols, :] = imag
    hr[:, dof:, :] = jnp.ones((dof, 8, lanes), jnp.float32)
    hi[:, dof:, :] = jnp.zeros((dof, 8, lanes), jnp.float32)
    xr[...] = jnp.zeros_like(xr)
    xi[...] = jnp.zeros_like(xi)
    sub = lax.broadcasted_iota(jnp.int32, (8, lanes), 0)

    for kb in range(nb):

        def step(k, carry, kb=kb):
            pivot = 1.0 / hr[k, pl.ds(k, 1), :]
            rr = [hr[k, 8 * b : 8 * b + 8, :] for b in range(kb, nb + 1)]
            ri = [hi[k, 8 * b : 8 * b + 8, :] for b in range(kb, nb + 1)]
            for ib in range(kb, nb):
                fr = rr[ib - kb] * pivot
                fi = -ri[ib - kb] * pivot
                if ib == kb:
                    live = sub + 8 * kb > k
                    fr = jnp.where(live, fr, 0.0)
                    fi = jnp.where(live, fi, 0.0)
                for s in range(8):
                    i = 8 * ib + s
                    cr = jnp.broadcast_to(fr[s : s + 1], (8, lanes))
                    ci = jnp.broadcast_to(fi[s : s + 1], (8, lanes))
                    for b in range(ib, nb + 1):
                        pr, pi = rr[b - kb], ri[b - kb]
                        sl = slice(8 * b, 8 * b + 8)
                        hr[i, sl, :] = hr[i, sl, :] - (cr * pr - ci * pi)
                        hi[i, sl, :] = hi[i, sl, :] - (cr * pi + ci * pr)
            return carry

        lax.fori_loop(8 * kb, 8 * kb + 8, step, 0)

    for ib in reversed(range(nb)):

        def back(t, carry, ib=ib):
            i = 8 * ib + 7 - t
            sr = jnp.zeros((8, lanes), jnp.float32)
            si = jnp.zeros((8, lanes), jnp.float32)
            for b in range(ib, nb):
                sl = slice(8 * b, 8 * b + 8)
                ar, ai = hr[i, sl, :], hi[i, sl, :]
                br, bi = xr[sl, :], xi[sl, :]
                sr = sr + (ar * br - ai * bi)
                si = si + (ar * bi + ai * br)
            pivot = 1.0 / hr[i, pl.ds(i, 1), :]
            top_r = hr[i, dof : dof + 1, :]
            top_i = hi[i, dof : dof + 1, :]
            xr[pl.ds(i, 1), :] = (top_r - jnp.sum(sr, 0, keepdims=True)) * pivot
            xi[pl.ds(i, 1), :] = (top_i - jnp.sum(si, 0, keepdims=True)) * pivot
            return carry

        lax.fori_loop(0, 8, back, 0)
    out_ref[:dof, :] = xr[...]
    out_ref[dof : 2 * dof, :] = xi[...]
    out_ref[2 * dof :, :] = jnp.broadcast_to(jnp.sum(xr[...], 0, keepdims=True), (8, lanes))


MESH = pl.DeviceIdType.MESH


def scatter_kernel(n, g_ref, out_ref, pair, acc, right, left, psend, precv, rsend, rrecv, lsend, lrecv):
    me = lax.axis_index("rng")
    z = me // 2
    c = me % 2
    mate = 2 * z + 1 - c
    ahead = lax.rem(me + 2, 2 * n)
    behind = lax.rem(me + 2 * n - 2, 2 * n)
    barrier = pltpu.get_barrier_semaphore()
    pl.semaphore_signal(barrier, inc=1, device_id={"rng": mate}, device_id_type=MESH)
    pl.semaphore_signal(barrier, inc=1, device_id={"rng": ahead}, device_id_type=MESH)
    pl.semaphore_signal(barrier, inc=1, device_id={"rng": behind}, device_id_type=MESH)
    pl.semaphore_wait(barrier, 3)

    order = []
    for t in range((n + 1) // 2):
        order.append(n - 1 - t)
        if t != n - 1 - t:
            order.append(t)

    def pair_copy(t):
        return pltpu.make_async_remote_copy(
            src_ref=g_ref.at[2 * t + 1 - c],
            dst_ref=pair.at[t],
            send_sem=psend.at[t],
            recv_sem=precv.at[t],
            device_id={"rng": mate},
            device_id_type=MESH,
        )

    def right_copy(t):
        return pltpu.make_async_remote_copy(
            src_ref=acc.at[t],
            dst_ref=right.at[t],
            send_sem=rsend.at[t],
            recv_sem=rrecv.at[t],
            device_id={"rng": ahead},
            device_id_type=MESH,
        )

    def left_copy(t):
        return pltpu.make_async_remote_copy(
            src_ref=acc.at[t],
            dst_ref=left.at[t],
            send_sem=lsend.at[t],
            recv_sem=lrecv.at[t],
            device_id={"rng": behind},
            device_id_type=MESH,
        )

    for t in order:
        pair_copy(t).start()
    for t in order:
        pair_copy(t).wait_recv()
        acc[t] = g_ref[2 * t + c] + pair[t]

        @pl.when(jnp.logical_and(z == 0, t > 0))
        def _(t=t):
            right_copy(t).start()

        @pl.when(jnp.logical_and(z == n - 1, t < n - 1))
        def _(t=t):
            left_copy(t).start()

    for place in range(n):
        events = [(place + n - 1 - t, 0, t) for t in range(place + 1, n) if place > 0]
        events += [(n - 1 - place + t, 1, t) for t in range(place) if place < n - 1]

        @pl.when(z == place)
        def _(place=place, events=sorted(events)):
            for _, side, t in events:
                copy = left_copy(t) if side else right_copy(t)
                source = left if side else right
                copy.wait_recv()
                acc[t] = acc[t] + source[t]
                copy.start()
            total = acc[place]
            if place > 0:
                right_copy(place).wait_recv()
                total = total + right[place]
            if place < n - 1:
                left_copy(place).wait_recv()
                total = total + left[place]
            out_ref[...] = total

    for t in range(n):
        pair_copy(t).wait_send()

        @pl.when(z < t)
        def _(t=t):
            right_copy(t).wait_send()

        @pl.when(z > t)
        def _(t=t):
            left_copy(t).wait_send()


def apply_kernel(
    halves,
    per,
    dof,
    pay_ref,
    bins_ref,
    *refs,
):
    v_refs = refs[:halves]
    (out_ref, v_all, gat, power, edge, halo, sums, az_lo, az_hi) = refs[halves : halves + 9]
    (vsem, gsend, grecv, esend, erecv, asend, arecv) = refs[halves + 9 :]
    me = lax.axis_index("rng")
    az = lax.axis_index("az")
    n = lax.axis_size("rng")
    m = lax.axis_size("az")
    beams, num_chan, cells = out_ref.shape
    pulses, num_sel = v_all.shape[2], v_all.shape[3]
    taps = pulses * num_sel
    az_next = lax.rem(az + 1, m)
    az_prev = lax.rem(az + m - 1, m)
    barrier = pltpu.get_barrier_semaphore()
    for d in range(1, n):
        peer = lax.rem(me + d, n)
        pl.semaphore_signal(barrier, inc=1, device_id={"rng": peer}, device_id_type=MESH)
    for other in (az_next, az_prev):
        pl.semaphore_signal(barrier, inc=1, device_id={"az": other}, device_id_type=MESH)
    share = beams // halves
    loads = []
    for h in range(halves):
        load = pltpu.make_async_copy(v_refs[h], v_all.at[pl.ds(h * share, share)], vsem.at[h])
        load.start()
        loads.append(load)
    pl.semaphore_wait(barrier, n + 1)

    copies = []
    for d in range(1, n):
        peer = lax.rem(me + d, n)
        copy = pltpu.make_async_remote_copy(
            src_ref=pay_ref,
            dst_ref=gat.at[me],
            send_sem=gsend.at[d],
            recv_sem=grecv.at[d],
            device_id={"rng": peer},
            device_id_type=MESH,
        )
        copy.start()
        copies.append(copy)
    gat[me] = pay_ref[...]
    for load in loads:
        load.wait()
    for copy in copies:
        copy.wait_recv()
    rows = gat.shape[1] - beams
    count = jnp.zeros((beams, gat.shape[2]), jnp.float32)
    for r in range(n):
        count = count + gat[r, rows:, :]
    sums[0] = jnp.zeros(sums.shape[1:], jnp.float32)
    for b in range(beams):
        sums[b, :1, :] = count[b : b + 1]
    freq = lax.broadcasted_iota(jnp.int32, (num_chan, taps), 1) // num_sel
    lanes = gat.shape[2]
    lane = lax.broadcasted_iota(jnp.int32, (num_chan, lanes), 1)

    def one(b, carry):
        if per >= num_chan:
            ratio = per // num_chan
            start = pl.multiple_of((b % ratio) * num_chan, 8)
            w = gat[b // ratio, pl.ds(start, num_chan), :]
        else:
            split = num_chan // per
            w = jnp.concatenate([gat[b * split + t, :per, :] for t in range(split)], 0)
        w = w * sums[b, :1, :]
        quiet = w[:, 2 * dof : 2 * dof + 1]
        centre = bins_ref[b]
        planes = []
        hits = []
        for q in range(BINS):
            f = lax.rem(centre + (q - BINS // 2 + pulses), pulses)
            hits.append(freq == f)
        for part in range(2):
            plane = jnp.zeros((num_chan, taps), jnp.float32)
            for q in range(BINS):
                start = part * dof + q * num_sel
                piece = pltpu.roll(w, (lanes - start) % lanes, 1) if start else w
                piece = jnp.where(lane < num_sel, piece, 0.0)
                span = num_sel
                while span < lanes:
                    piece = piece + pltpu.roll(piece, span, 1)
                    span *= 2
                tiled = jnp.concatenate([piece] * (taps // lanes), 1)
                plane = jnp.where(hits[q], tiled, plane)
            planes.append(plane)
        top = jnp.concatenate([planes[0], planes[1]], 1)
        low = jnp.concatenate([-planes[1], planes[0]], 1)
        lhs = jnp.concatenate([top, low], 0).astype(jnp.bfloat16)
        flat = v_all[b].reshape(2 * taps, cells)
        proj = jnp.dot(lhs, flat, preferred_element_type=jnp.float32)
        p0 = proj[:num_chan]
        p1 = proj[num_chan:]
        power[b] = (p0 * p0 + p1 * p1) / quiet
        return carry

    lax.fori_loop(0, beams, one, 0)
    items = beams * num_chan
    turned = power[...].reshape(items, cells).T
    edge[0] = turned[:8]
    edge[1] = turned[cells - 8 :]

    def edge_copy(side):
        target = lax.rem(me + 1, n) if side else lax.rem(me + n - 1, n)
        return pltpu.make_async_remote_copy(
            src_ref=edge.at[side],
            dst_ref=halo.at[side],
            send_sem=esend.at[side],
            recv_sem=erecv.at[side],
            device_id={"rng": target},
            device_id_type=MESH,
        )

    for side in range(2):
        edge_copy(side).start()
    for side in range(2):
        edge_copy(side).wait()
    before = jnp.where(me > 0, halo[1, 7:8], 0.0)
    after = jnp.where(me < n - 1, halo[0, 0:1], 0.0)
    turned = (
        jnp.concatenate([before, turned[:-1]], 0)
        + turned
        + jnp.concatenate([turned[1:], after], 0)
    )
    sums[...] = turned.T.reshape(beams, num_chan, cells)
    up = pltpu.make_async_remote_copy(
        src_ref=sums.at[beams - 1],
        dst_ref=az_lo,
        send_sem=asend.at[0],
        recv_sem=arecv.at[0],
        device_id={"az": az_next},
        device_id_type=MESH,
    )
    down = pltpu.make_async_remote_copy(
        src_ref=sums.at[0],
        dst_ref=az_hi,
        send_sem=asend.at[1],
        recv_sem=arecv.at[1],
        device_id={"az": az_prev},
        device_id_type=MESH,
    )
    up.start()
    down.start()
    for b in range(1, beams - 1):
        out_ref[b] = (sums[b - 1] + sums[b] + sums[b + 1]) / 9.0
    up.wait_recv()
    down.wait_recv()
    out_ref[0] = (az_lo[...] + sums[0] + sums[1]) / 9.0
    out_ref[beams - 1] = (sums[beams - 2] + sums[beams - 1] + az_hi[...]) / 9.0
    up.wait_send()
    down.wait_send()
    for copy in copies:
        copy.wait_send()


def body(echoes, arc_start, arc_offsets, doppler_bins, steer_angles, train_mask):
    columns = echoes.shape[1]
    num_pulses = echoes.shape[2]
    cells = echoes.shape[3]
    num_sel = arc_offsets.shape[1]
    chan_count = doppler_bins.shape[1]
    cycle_size = lax.axis_size("az")
    cycle_pos = lax.axis_index("az")
    rng_size = lax.axis_size("rng")
    beam_count = BEAMS // cycle_size
    item_count = beam_count * chan_count
    dof = BINS * num_sel
    table_re, table_im = doppler_table(num_pulses)
    table = jnp.concatenate(
        [jnp.concatenate([table_re, -table_im], 1), jnp.concatenate([table_im, table_re], 1)], 0
    )

    def own(x):
        return lax.dynamic_slice_in_dim(x, cycle_pos * beam_count, beam_count, axis=0)

    arc_first = (own(arc_start) - cycle_pos * columns + ARC // 2) % COLS
    col_index = arc_first[:, None] + own(arc_offsets)
    bins_own = own(doppler_bins)
    angles = own(steer_angles)
    block_count = train_mask.shape[1]
    cell_mask = (
        jnp.broadcast_to(train_mask[:, :, None], (beam_count, block_count, BLK))
        .reshape(beam_count, 1, block_count * BLK)
        .astype(jnp.bfloat16)
    )
    smem = pl.BlockSpec(memory_space=pltpu.SMEM)

    def snap_gram(extended, first, last, base):
        share = last - first
        ext_cols = extended.shape[1]
        return pl.pallas_call(
            snap_gram_kernel,
            grid=(share,),
            in_specs=[
                smem,
                smem,
                smem,
                smem,
                pl.BlockSpec((2, ext_cols, num_pulses, cells), lambda b: (0, 0, 0, 0)),
                pl.BlockSpec(table.shape, lambda b: (0, 0)),
                pl.BlockSpec((1, 1, cells), lambda b: (b, 0, 0)),
            ],
            out_specs=[
                pl.BlockSpec((1, 2, num_pulses, num_sel, cells), lambda b: (b, 0, 0, 0, 0)),
                pl.BlockSpec((1, dof, chan_count * dof), lambda b: (b, 0, 0)),
            ],
            out_shape=[
                jax.ShapeDtypeStruct((share, 2, num_pulses, num_sel, cells), jnp.bfloat16),
                jax.ShapeDtypeStruct((share, dof, chan_count * dof), jnp.float32),
            ],
            compiler_params=pltpu.CompilerParams(vmem_limit_bytes=VMEM_LIMIT),
            cost_estimate=pl.CostEstimate(
                flops=share * 600_000_000, bytes_accessed=share * 1_500_000, transcendentals=0
            ),
            name="snap_gram",
        )(
            col_index[first:last] - base,
            bins_own[first:last],
            jnp.cos(angles)[first:last],
            jnp.sin(angles)[first:last],
            extended,
            table,
            cell_mask[first:last],
        )

    width = ARC // 2
    forward = [(i, (i + 1) % cycle_size) for i in range(cycle_size)]
    backward = [(target, source) for source, target in forward]
    low = lax.ppermute(echoes[:, columns - width :], "az", forward)
    high = lax.ppermute(echoes[:, :width], "az", backward)
    step = COLS // BEAMS
    half = beam_count // 2
    if (half - 1) * step + step - 1 + ARC - 1 < width + columns and half * step >= width:
        v_lo, gram_lo = snap_gram(jnp.concatenate([low, echoes], 1), 0, half, 0)
        high, v_lo, gram_lo = lax.optimization_barrier((high, v_lo, gram_lo))
        v_hi, gram_hi = snap_gram(jnp.concatenate([echoes, high], 1), half, beam_count, width)
        v_parts = (v_lo, v_hi)
        gram = jnp.concatenate([gram_lo, gram_hi], 0)
    else:
        v_one, gram = snap_gram(jnp.concatenate([low, echoes, high], 1), 0, beam_count, 0)
        v_parts = (v_one,)

    per = item_count // rng_size
    if per < chan_count:
        split = chan_count // per
        gram = gram.reshape(beam_count, dof, split, per * dof)
        gram = jnp.swapaxes(gram, 1, 2).reshape(beam_count * split, dof, per * dof)
        width = per
    else:
        width = chan_count
    vm = pltpu.VMEM
    dma = pltpu.SemaphoreType.DMA
    line = rng_size // 2
    chunk = (gram.shape[0] // rng_size, dof, gram.shape[2])
    part = pl.pallas_call(
        functools.partial(scatter_kernel, line),
        in_specs=[pl.BlockSpec(memory_space=vm)],
        out_specs=pl.BlockSpec(memory_space=vm),
        out_shape=jax.ShapeDtypeStruct(chunk, jnp.float32),
        scratch_shapes=[vm((line,) + chunk, jnp.float32)] * 4 + [dma((line,))] * 6,
        compiler_params=pltpu.CompilerParams(
            collective_id=0, has_side_effects=True, vmem_limit_bytes=VMEM_LIMIT
        ),
        name="scatter",
    )(gram.reshape((rng_size,) + chunk))
    solved = pl.pallas_call(
        solve_kernel,
        out_shape=jax.ShapeDtypeStruct((2 * dof + 8, per), jnp.float32),
        scratch_shapes=[
            vm((dof, per, dof), jnp.float32),
            vm((dof, dof, per), jnp.float32),
            vm((dof, dof + 8, per), jnp.float32),
            vm((dof, dof + 8, per), jnp.float32),
            vm((dof, per), jnp.float32),
            vm((dof, per), jnp.float32),
        ],
        compiler_params=pltpu.CompilerParams(vmem_limit_bytes=VMEM_LIMIT),
        name="solve",
    )(part)
    lanes = 128
    local_count = (BLK * jnp.sum(train_mask, axis=1)).astype(jnp.float32)
    pad_rows = -per % 8
    payload = jnp.concatenate(
        [
            jnp.pad(solved.T, ((0, pad_rows), (0, lanes - solved.shape[0]))),
            jnp.broadcast_to(local_count[:, None], (beam_count, lanes)),
        ],
        0,
    )
    halves = len(v_parts)
    any_spec = pl.BlockSpec(memory_space=pl.ANY)
    block = (chan_count, cells)
    out = pl.pallas_call(
        functools.partial(apply_kernel, halves, per, dof),
        in_specs=[pl.BlockSpec(memory_space=vm)] * 2 + [any_spec] * halves,
        out_specs=pl.BlockSpec(memory_space=vm),
        out_shape=jax.ShapeDtypeStruct((beam_count,) + block, jnp.float32),
        scratch_shapes=[
            vm((beam_count, 2, num_pulses, num_sel, cells), jnp.bfloat16),
            vm((rng_size,) + payload.shape, jnp.float32),
            vm((beam_count,) + block, jnp.float32),
            vm((2, 8, item_count), jnp.float32),
            vm((2, 8, item_count), jnp.float32),
            vm((beam_count,) + block, jnp.float32),
            vm(block, jnp.float32),
            vm(block, jnp.float32),
            dma((halves,)),
            dma((rng_size,)),
            dma((rng_size,)),
            dma((2,)),
            dma((2,)),
            dma((2,)),
            dma((2,)),
        ],
        compiler_params=pltpu.CompilerParams(
            collective_id=1, has_side_effects=True, vmem_limit_bytes=VMEM_LIMIT
        ),
        name="apply",
    )(payload, bins_own[:, :, None], *v_parts)
    return out


def solution(mesh):
    return jax.shard_map(
        body,
        mesh=mesh,
        in_specs=(P(None, "az", None, "rng"), P(), P(), P(), P(), P("az", "rng")),
        out_specs=P("az", None, "rng"),
        check_vma=False,
    )
```

```python
import functools

import jax
import jax.numpy as jnp
from jax import lax
from jax.experimental import pallas as pl
from jax.experimental.pallas import tpu as pltpu
from jax.sharding import PartitionSpec as P


COLS = 256
ARC = 64
BINS = 3
BEAMS = 64
BLK = 128
LOADING = 0.1
VMEM_LIMIT = 48 << 20


def doppler_table(num_pulses):
    freq_ids = jnp.arange(num_pulses, dtype=jnp.int32)
    phase_steps = freq_ids[:, None] * freq_ids[None, :] % num_pulses
    phase_angle = -2.0 * jnp.pi / num_pulses * phase_steps.astype(jnp.float32)
    return (jnp.cos(phase_angle).astype(jnp.bfloat16), jnp.sin(phase_angle).astype(jnp.bfloat16))


def snap_gram_kernel(
    col_ref, bins_ref, cos_ref, sin_ref, ext_ref, table_ref, mask_ref, v_ref, gram_ref
):
    beam = pl.program_id(0)
    pulses = ext_ref.shape[2]
    num_sel = col_ref.shape[1]
    num_chan = bins_ref.shape[1]
    table = table_ref[...]
    parts_re, parts_im = [], []
    for j in range(num_sel):
        col = col_ref[beam, j]
        data = jnp.concatenate([ext_ref[0, col], ext_ref[1, col]], axis=0)
        spec = jnp.dot(table, data, preferred_element_type=jnp.float32)
        cosine = cos_ref[beam, j]
        sine = sin_ref[beam, j]
        spec_re = spec[:pulses]
        spec_im = spec[pulses:]
        parts_re.append(cosine * spec_re - sine * spec_im)
        parts_im.append(sine * spec_re + cosine * spec_im)
    for part, pieces in enumerate((parts_re, parts_im)):
        stacked = jnp.swapaxes(jnp.stack(pieces, 0), 0, 1)
        v_ref[0, part] = stacked.astype(jnp.bfloat16)
    dof = BINS * num_sel
    mask_row = mask_ref[0]
    row = lax.broadcasted_iota(jnp.int32, (dof, dof), 0)
    colm = lax.broadcasted_iota(jnp.int32, (dof, dof), 1)
    lower = row >= colm
    packed = []
    for k in range(num_chan):
        centre = bins_ref[beam, k]
        ids = [(centre + (q - BINS // 2 + pulses)) % pulses for q in range(BINS)]
        u_re = jnp.concatenate([v_ref[0, 0, f] for f in ids], 0)
        u_im = jnp.concatenate([v_ref[0, 1, f] for f in ids], 0)
        right = jnp.concatenate([u_re, u_im], 1)
        m_re = u_re * mask_row
        m_im = u_im * mask_row
        left = jnp.concatenate(
            [jnp.concatenate([m_re, m_im], 1), jnp.concatenate([m_im, -m_re], 1)], 0
        )
        both = lax.dot_general(
            left, right, (((1,), (1,)), ((), ())), preferred_element_type=jnp.float32
        )
        packed.append(jnp.where(lower, both[:dof], both[dof:]))
    gram_ref[0] = jnp.concatenate(packed, 1)


def solve_kernel(part_ref, out_ref, stack, turned, hr, hi, xr, xi):
    lead, dof, wide = part_ref.shape
    width = wide // dof
    lanes = lead * width
    nb = dof // 8
    group = min(8, lanes)
    for g in range(0, lanes, group):
        pieces = []
        for item in range(g, g + group):
            k = item % width
            pieces.append(part_ref[item // width, :, k * dof : (k + 1) * dof])
        stack[:, g : g + group, :] = jnp.swapaxes(jnp.stack(pieces, 0), 0, 1)
    for i in range(dof):
        turned[i] = stack[i].T
    trace = jnp.zeros((1, lanes), jnp.float32)
    for i in range(dof):
        trace = trace + turned[i, i : i + 1, :]
    load = (LOADING / dof) * trace
    cube = (8, 8, lanes)
    row = lax.broadcasted_iota(jnp.int32, cube, 0)
    col = lax.broadcasted_iota(jnp.int32, cube, 1)
    for ib in range(nb):
        rows = slice(8 * ib, 8 * ib + 8)
        for jb in range(ib, nb):
            cols = slice(8 * jb, 8 * jb + 8)
            imag = turned[rows, cols, :]
            real = jnp.swapaxes(turned[cols, rows, :], 0, 1)
            if ib == jb:
                straight, flip = imag, real
                real = jnp.where(row >= col, straight, flip)
                real = jnp.where(row == col, real + load[None], real)
                imag = jnp.where(row < col, straight, jnp.where(row > col, -flip, 0.0))
            hr[rows, cols, :] = real
            hi[rows, cols, :] = imag
    hr[:, dof:, :] = jnp.ones((dof, 8, lanes), jnp.float32)
    hi[:, dof:, :] = jnp.zeros((dof, 8, lanes), jnp.float32)
    xr[...] = jnp.zeros_like(xr)
    xi[...] = jnp.zeros_like(xi)
    sub = lax.broadcasted_iota(jnp.int32, (8, lanes), 0)

    for kb in range(nb):

        def step(k, carry, kb=kb):
            pivot = 1.0 / hr[k, pl.ds(k, 1), :]
            rr = [hr[k, 8 * b : 8 * b + 8, :] for b in range(kb, nb + 1)]
            ri = [hi[k, 8 * b : 8 * b + 8, :] for b in range(kb, nb + 1)]
            for ib in range(kb, nb):
                fr = rr[ib - kb] * pivot
                fi = -ri[ib - kb] * pivot
                if ib == kb:
                    live = sub + 8 * kb > k
                    fr = jnp.where(live, fr, 0.0)
                    fi = jnp.where(live, fi, 0.0)
                for s in range(8):
                    i = 8 * ib + s
                    cr = jnp.broadcast_to(fr[s : s + 1], (8, lanes))
                    ci = jnp.broadcast_to(fi[s : s + 1], (8, lanes))
                    for b in range(ib, nb + 1):
                        pr, pi = rr[b - kb], ri[b - kb]
                        sl = slice(8 * b, 8 * b + 8)
                        hr[i, sl, :] = hr[i, sl, :] - (cr * pr - ci * pi)
                        hi[i, sl, :] = hi[i, sl, :] - (cr * pi + ci * pr)
            return carry

        lax.fori_loop(8 * kb, 8 * kb + 8, step, 0)

    for ib in reversed(range(nb)):

        def back(t, carry, ib=ib):
            i = 8 * ib + 7 - t
            sr = jnp.zeros((8, lanes), jnp.float32)
            si = jnp.zeros((8, lanes), jnp.float32)
            for b in range(ib, nb):
                sl = slice(8 * b, 8 * b + 8)
                ar, ai = hr[i, sl, :], hi[i, sl, :]
                br, bi = xr[sl, :], xi[sl, :]
                sr = sr + (ar * br - ai * bi)
                si = si + (ar * bi + ai * br)
            pivot = 1.0 / hr[i, pl.ds(i, 1), :]
            top_r = hr[i, dof : dof + 1, :]
            top_i = hi[i, dof : dof + 1, :]
            xr[pl.ds(i, 1), :] = (top_r - jnp.sum(sr, 0, keepdims=True)) * pivot
            xi[pl.ds(i, 1), :] = (top_i - jnp.sum(si, 0, keepdims=True)) * pivot
            return carry

        lax.fori_loop(0, 8, back, 0)
    out_ref[:dof, :] = xr[...]
    out_ref[dof : 2 * dof, :] = xi[...]
    out_ref[2 * dof :, :] = jnp.broadcast_to(jnp.sum(xr[...], 0, keepdims=True), (8, lanes))


MESH = pl.DeviceIdType.MESH


def scatter_kernel(n, halves, *refs):
    g_refs = refs[:halves]
    out_ref, pair, acc, right, left, psend, precv, rsend, rrecv, lsend, lrecv = refs[halves:]
    share = n // halves

    def own(t, core):
        return g_refs[t // share].at[2 * (t % share) + core]

    me = lax.axis_index("rng")
    z = me // 2
    c = me % 2
    mate = 2 * z + 1 - c
    ahead = lax.rem(me + 2, 2 * n)
    behind = lax.rem(me + 2 * n - 2, 2 * n)
    barrier = pltpu.get_barrier_semaphore()
    pl.semaphore_signal(barrier, inc=1, device_id={"rng": mate}, device_id_type=MESH)
    pl.semaphore_signal(barrier, inc=1, device_id={"rng": ahead}, device_id_type=MESH)
    pl.semaphore_signal(barrier, inc=1, device_id={"rng": behind}, device_id_type=MESH)
    pl.semaphore_wait(barrier, 3)

    order = []
    for t in range((n + 1) // 2):
        order.append(n - 1 - t)
        if t != n - 1 - t:
            order.append(t)

    def pair_copy(t):
        return pltpu.make_async_remote_copy(
            src_ref=own(t, 1 - c),
            dst_ref=pair.at[t],
            send_sem=psend.at[t],
            recv_sem=precv.at[t],
            device_id={"rng": mate},
            device_id_type=MESH,
        )

    def right_copy(t):
        return pltpu.make_async_remote_copy(
            src_ref=acc.at[t],
            dst_ref=right.at[t],
            send_sem=rsend.at[t],
            recv_sem=rrecv.at[t],
            device_id={"rng": ahead},
            device_id_type=MESH,
        )

    def left_copy(t):
        return pltpu.make_async_remote_copy(
            src_ref=acc.at[t],
            dst_ref=left.at[t],
            send_sem=lsend.at[t],
            recv_sem=lrecv.at[t],
            device_id={"rng": behind},
            device_id_type=MESH,
        )

    for t in order:
        pair_copy(t).start()
    for t in order:
        pair_copy(t).wait_recv()
        acc[t] = own(t, c)[...] + pair[t]

        @pl.when(jnp.logical_and(z == 0, t > 0))
        def _(t=t):
            right_copy(t).start()

        @pl.when(jnp.logical_and(z == n - 1, t < n - 1))
        def _(t=t):
            left_copy(t).start()

    for place in range(n):
        events = [(place + n - 1 - t, 0, t) for t in range(place + 1, n) if place > 0]
        events += [(n - 1 - place + t, 1, t) for t in range(place) if place < n - 1]

        @pl.when(z == place)
        def _(place=place, events=sorted(events)):
            for _, side, t in events:
                copy = left_copy(t) if side else right_copy(t)
                source = left if side else right
                copy.wait_recv()
                acc[t] = acc[t] + source[t]
                copy.start()
            total = acc[place]
            if place > 0:
                right_copy(place).wait_recv()
                total = total + right[place]
            if place < n - 1:
                left_copy(place).wait_recv()
                total = total + left[place]
            out_ref[...] = total

    for t in range(n):
        pair_copy(t).wait_send()

        @pl.when(z < t)
        def _(t=t):
            right_copy(t).wait_send()

        @pl.when(z > t)
        def _(t=t):
            left_copy(t).wait_send()


def apply_kernel(
    halves,
    per,
    dof,
    pay_ref,
    bins_ref,
    *refs,
):
    v_refs = refs[:halves]
    (out_ref, v_all, gat, power, edge, halo, sums, az_lo, az_hi) = refs[halves : halves + 9]
    (vsem, gsend, grecv, esend, erecv, asend, arecv) = refs[halves + 9 :]
    me = lax.axis_index("rng")
    az = lax.axis_index("az")
    n = lax.axis_size("rng")
    m = lax.axis_size("az")
    beams, num_chan, cells = out_ref.shape
    pulses, num_sel = v_all.shape[2], v_all.shape[3]
    taps = pulses * num_sel
    az_next = lax.rem(az + 1, m)
    az_prev = lax.rem(az + m - 1, m)
    barrier = pltpu.get_barrier_semaphore()
    for d in range(1, n):
        peer = lax.rem(me + d, n)
        pl.semaphore_signal(barrier, inc=1, device_id={"rng": peer}, device_id_type=MESH)
    for other in (az_next, az_prev):
        pl.semaphore_signal(barrier, inc=1, device_id={"az": other}, device_id_type=MESH)
    share = beams // halves
    loads = []
    for h in range(halves):
        load = pltpu.make_async_copy(v_refs[h], v_all.at[pl.ds(h * share, share)], vsem.at[h])
        load.start()
        loads.append(load)
    pl.semaphore_wait(barrier, n + 1)

    copies = []
    for d in range(1, n):
        peer = lax.rem(me + d, n)
        copy = pltpu.make_async_remote_copy(
            src_ref=pay_ref,
            dst_ref=gat.at[me],
            send_sem=gsend.at[d],
            recv_sem=grecv.at[d],
            device_id={"rng": peer},
            device_id_type=MESH,
        )
        copy.start()
        copies.append(copy)
    gat[me] = pay_ref[...]
    for load in loads:
        load.wait()
    for copy in copies:
        copy.wait_recv()
    rows = gat.shape[1] - beams
    count = jnp.zeros((beams, gat.shape[2]), jnp.float32)
    for r in range(n):
        count = count + gat[r, rows:, :]
    sums[0] = jnp.zeros(sums.shape[1:], jnp.float32)
    for b in range(beams):
        sums[b, :1, :] = count[b : b + 1]
    freq = lax.broadcasted_iota(jnp.int32, (num_chan, taps), 1) // num_sel
    lanes = gat.shape[2]
    lane = lax.broadcasted_iota(jnp.int32, (num_chan, lanes), 1)

    def one(b, carry):
        if per >= num_chan:
            ratio = per // num_chan
            start = pl.multiple_of((b % ratio) * num_chan, 8)
            w = gat[b // ratio, pl.ds(start, num_chan), :]
        else:
            split = num_chan // per
            w = jnp.concatenate([gat[b * split + t, :per, :] for t in range(split)], 0)
        w = w * sums[b, :1, :]
        quiet = w[:, 2 * dof : 2 * dof + 1]
        centre = bins_ref[b]
        planes = []
        hits = []
        for q in range(BINS):
            f = lax.rem(centre + (q - BINS // 2 + pulses), pulses)
            hits.append(freq == f)
        for part in range(2):
            plane = jnp.zeros((num_chan, taps), jnp.float32)
            for q in range(BINS):
                start = part * dof + q * num_sel
                piece = pltpu.roll(w, (lanes - start) % lanes, 1) if start else w
                piece = jnp.where(lane < num_sel, piece, 0.0)
                span = num_sel
                while span < lanes:
                    piece = piece + pltpu.roll(piece, span, 1)
                    span *= 2
                tiled = jnp.concatenate([piece] * (taps // lanes), 1)
                plane = jnp.where(hits[q], tiled, plane)
            planes.append(plane)
        top = jnp.concatenate([planes[0], planes[1]], 1)
        low = jnp.concatenate([-planes[1], planes[0]], 1)
        lhs = jnp.concatenate([top, low], 0).astype(jnp.bfloat16)
        flat = v_all[b].reshape(2 * taps, cells)
        proj = jnp.dot(lhs, flat, preferred_element_type=jnp.float32)
        p0 = proj[:num_chan]
        p1 = proj[num_chan:]
        power[b] = (p0 * p0 + p1 * p1) / quiet
        return carry

    lax.fori_loop(0, beams, one, 0)
    items = beams * num_chan
    turned = power[...].reshape(items, cells).T
    edge[0] = turned[:8]
    edge[1] = turned[cells - 8 :]

    def edge_copy(side):
        target = lax.rem(me + 1, n) if side else lax.rem(me + n - 1, n)
        return pltpu.make_async_remote_copy(
            src_ref=edge.at[side],
            dst_ref=halo.at[side],
            send_sem=esend.at[side],
            recv_sem=erecv.at[side],
            device_id={"rng": target},
            device_id_type=MESH,
        )

    for side in range(2):
        edge_copy(side).start()
    for side in range(2):
        edge_copy(side).wait()
    before = jnp.where(me > 0, halo[1, 7:8], 0.0)
    after = jnp.where(me < n - 1, halo[0, 0:1], 0.0)
    turned = (
        jnp.concatenate([before, turned[:-1]], 0)
        + turned
        + jnp.concatenate([turned[1:], after], 0)
    )
    sums[...] = turned.T.reshape(beams, num_chan, cells)
    up = pltpu.make_async_remote_copy(
        src_ref=sums.at[beams - 1],
        dst_ref=az_lo,
        send_sem=asend.at[0],
        recv_sem=arecv.at[0],
        device_id={"az": az_next},
        device_id_type=MESH,
    )
    down = pltpu.make_async_remote_copy(
        src_ref=sums.at[0],
        dst_ref=az_hi,
        send_sem=asend.at[1],
        recv_sem=arecv.at[1],
        device_id={"az": az_prev},
        device_id_type=MESH,
    )
    up.start()
    down.start()
    for b in range(1, beams - 1):
        out_ref[b] = (sums[b - 1] + sums[b] + sums[b + 1]) / 9.0
    up.wait_recv()
    down.wait_recv()
    out_ref[0] = (az_lo[...] + sums[0] + sums[1]) / 9.0
    out_ref[beams - 1] = (sums[beams - 2] + sums[beams - 1] + az_hi[...]) / 9.0
    up.wait_send()
    down.wait_send()
    for copy in copies:
        copy.wait_send()


def body(echoes, arc_start, arc_offsets, doppler_bins, steer_angles, train_mask):
    columns = echoes.shape[1]
    num_pulses = echoes.shape[2]
    cells = echoes.shape[3]
    num_sel = arc_offsets.shape[1]
    chan_count = doppler_bins.shape[1]
    cycle_size = lax.axis_size("az")
    cycle_pos = lax.axis_index("az")
    rng_size = lax.axis_size("rng")
    beam_count = BEAMS // cycle_size
    item_count = beam_count * chan_count
    dof = BINS * num_sel
    table_re, table_im = doppler_table(num_pulses)
    table = jnp.concatenate(
        [jnp.concatenate([table_re, -table_im], 1), jnp.concatenate([table_im, table_re], 1)], 0
    )

    def own(x):
        return lax.dynamic_slice_in_dim(x, cycle_pos * beam_count, beam_count, axis=0)

    arc_first = (own(arc_start) - cycle_pos * columns + ARC // 2) % COLS
    col_index = arc_first[:, None] + own(arc_offsets)
    bins_own = own(doppler_bins)
    angles = own(steer_angles)
    block_count = train_mask.shape[1]
    cell_mask = (
        jnp.broadcast_to(train_mask[:, :, None], (beam_count, block_count, BLK))
        .reshape(beam_count, 1, block_count * BLK)
        .astype(jnp.bfloat16)
    )
    smem = pl.BlockSpec(memory_space=pltpu.SMEM)

    def snap_gram(extended, first, last, base):
        share = last - first
        ext_cols = extended.shape[1]
        return pl.pallas_call(
            snap_gram_kernel,
            grid=(share,),
            in_specs=[
                smem,
                smem,
                smem,
                smem,
                pl.BlockSpec((2, ext_cols, num_pulses, cells), lambda b: (0, 0, 0, 0)),
                pl.BlockSpec(table.shape, lambda b: (0, 0)),
                pl.BlockSpec((1, 1, cells), lambda b: (b, 0, 0)),
            ],
            out_specs=[
                pl.BlockSpec((1, 2, num_pulses, num_sel, cells), lambda b: (b, 0, 0, 0, 0)),
                pl.BlockSpec((1, dof, chan_count * dof), lambda b: (b, 0, 0)),
            ],
            out_shape=[
                jax.ShapeDtypeStruct((share, 2, num_pulses, num_sel, cells), jnp.bfloat16),
                jax.ShapeDtypeStruct((share, dof, chan_count * dof), jnp.float32),
            ],
            compiler_params=pltpu.CompilerParams(vmem_limit_bytes=VMEM_LIMIT),
            cost_estimate=pl.CostEstimate(
                flops=share * 600_000_000, bytes_accessed=share * 1_500_000, transcendentals=0
            ),
            name="snap_gram",
        )(
            col_index[first:last] - base,
            bins_own[first:last],
            jnp.cos(angles)[first:last],
            jnp.sin(angles)[first:last],
            extended,
            table,
            cell_mask[first:last],
        )

    width = ARC // 2
    forward = [(i, (i + 1) % cycle_size) for i in range(cycle_size)]
    backward = [(target, source) for source, target in forward]
    low = lax.ppermute(echoes[:, columns - width :], "az", forward)
    high = lax.ppermute(echoes[:, :width], "az", backward)
    step = COLS // BEAMS
    half = beam_count // 2
    if (half - 1) * step + step - 1 + ARC - 1 < width + columns and half * step >= width:
        v_lo, gram_lo = snap_gram(jnp.concatenate([low, echoes], 1), 0, half, 0)
        high, v_lo, gram_lo = lax.optimization_barrier((high, v_lo, gram_lo))
        v_hi, gram_hi = snap_gram(jnp.concatenate([echoes, high], 1), half, beam_count, width)
        v_parts = (v_lo, v_hi)
        grams = (gram_lo, gram_hi)
        if rng_size % 4 or item_count // rng_size < chan_count:
            grams = (jnp.concatenate(grams, 0),)
    else:
        v_one, gram_one = snap_gram(jnp.concatenate([low, echoes, high], 1), 0, beam_count, 0)
        v_parts = (v_one,)
        grams = (gram_one,)

    per = item_count // rng_size
    if per < chan_count:
        split = chan_count // per
        gram = grams[0].reshape(beam_count, dof, split, per * dof)
        grams = (jnp.swapaxes(gram, 1, 2).reshape(beam_count * split, dof, per * dof),)
        width = per
    else:
        width = chan_count
    vm = pltpu.VMEM
    dma = pltpu.SemaphoreType.DMA
    line = rng_size // 2
    chunk = (grams[0].shape[0] * len(grams) // rng_size, dof, grams[0].shape[2])
    part = pl.pallas_call(
        functools.partial(scatter_kernel, line, len(grams)),
        in_specs=[pl.BlockSpec(memory_space=vm)] * len(grams),
        out_specs=pl.BlockSpec(memory_space=vm),
        out_shape=jax.ShapeDtypeStruct(chunk, jnp.float32),
        scratch_shapes=[vm((line,) + chunk, jnp.float32)] * 4 + [dma((line,))] * 6,
        compiler_params=pltpu.CompilerParams(
            collective_id=0, has_side_effects=True, vmem_limit_bytes=VMEM_LIMIT
        ),
        name="scatter",
    )(*[g.reshape((rng_size // len(grams),) + chunk) for g in grams])
    solved = pl.pallas_call(
        solve_kernel,
        out_shape=jax.ShapeDtypeStruct((2 * dof + 8, per), jnp.float32),
        scratch_shapes=[
            vm((dof, per, dof), jnp.float32),
            vm((dof, dof, per), jnp.float32),
            vm((dof, dof + 8, per), jnp.float32),
            vm((dof, dof + 8, per), jnp.float32),
            vm((dof, per), jnp.float32),
            vm((dof, per), jnp.float32),
        ],
        compiler_params=pltpu.CompilerParams(vmem_limit_bytes=VMEM_LIMIT),
        name="solve",
    )(part)
    lanes = 128
    local_count = (BLK * jnp.sum(train_mask, axis=1)).astype(jnp.float32)
    pad_rows = -per % 8
    payload = jnp.concatenate(
        [
            jnp.pad(solved.T, ((0, pad_rows), (0, lanes - solved.shape[0]))),
            jnp.broadcast_to(local_count[:, None], (beam_count, lanes)),
        ],
        0,
    )
    halves = len(v_parts)
    any_spec = pl.BlockSpec(memory_space=pl.ANY)
    block = (chan_count, cells)
    out = pl.pallas_call(
        functools.partial(apply_kernel, halves, per, dof),
        in_specs=[pl.BlockSpec(memory_space=vm)] * 2 + [any_spec] * halves,
        out_specs=pl.BlockSpec(memory_space=vm),
        out_shape=jax.ShapeDtypeStruct((beam_count,) + block, jnp.float32),
        scratch_shapes=[
            vm((beam_count, 2, num_pulses, num_sel, cells), jnp.bfloat16),
            vm((rng_size,) + payload.shape, jnp.float32),
            vm((beam_count,) + block, jnp.float32),
            vm((2, 8, item_count), jnp.float32),
            vm((2, 8, item_count), jnp.float32),
            vm((beam_count,) + block, jnp.float32),
            vm(block, jnp.float32),
            vm(block, jnp.float32),
            dma((halves,)),
            dma((rng_size,)),
            dma((rng_size,)),
            dma((2,)),
            dma((2,)),
            dma((2,)),
            dma((2,)),
        ],
        compiler_params=pltpu.CompilerParams(
            collective_id=1, has_side_effects=True, vmem_limit_bytes=VMEM_LIMIT
        ),
        name="apply",
    )(payload, bins_own[:, :, None], *v_parts)
    return out


def solution(mesh):
    return jax.shard_map(
        body,
        mesh=mesh,
        in_specs=(P(None, "az", None, "rng"), P(), P(), P(), P(), P("az", "rng")),
        out_specs=P("az", None, "rng"),
        check_vma=False,
    )
```
